512 devices in a mesh: pairs: 128 (over x, z, core), ints: 4 (over y).
Axes of the slice: x: 4, y: 4, z: 16, core: 2. Of those that a mesh axis runs over, the one named last changes fastest.
Arguments:
- amps: float32 [256, 256, 256], P('pairs', 'ints'), may hold values from -0.8 to 0.8
- resid_rest: float32 [256, 256, 256], P('pairs', 'ints'), may hold values from -6 to 6
- int_blocks: bfloat16 [128, 256, 256], P('pairs'), may hold values from -0.375 to 0.375
- virt_energy: float32 [256, 256], P('pairs'), may hold values from 0.5 to 3
- pair_energy: float32 [256], P('pairs'), may hold values from -2 to -0.5
- item_block: int32 [32768, 1], P(('pairs', 'ints')), may hold values from 0 to 127; in each aligned block of 64 rows (0 to 63, 64 to 127, ...) at most 2 rows name the same one
- share_owner: int32 [12288, 1], P('pairs'), may hold values from 0 to 127; in each aligned block of 96 rows (0 to 95, 96 to 191, ...) at most 2 rows name the same one
- share_pair: int32 [12288, 1], P('pairs'), may hold values from 0 to 1
- share_amp: int32 [12288, 1], P('pairs'), may hold values from 0 to 1
- transpose_pair: int32 [256], P('pairs'), may hold values from 0 to 255, as said below
Outputs:
- update: float32 [256, 256, 256], P('pairs', 'ints')
The draws below stay inside these ranges and needn't reach their ends.
Inputs may be any that keep to these rules, and one draw needn't show every extreme that they name: `item_block`: within each aligned block of 64 rows no value occurs more than 2 times, and some value occurs exactly 2 times. `share_owner`: within each aligned block of 96 rows no value occurs more than 2 times, and some value occurs exactly 2 times. `transpose_pair`: A permutation equal to its own inverse; pair p maps into the block of 2 consecutive pairs whose block number is (p // 2 + 256 // 4) modulo 256 // 2.
All inputs are finite; a program needn't handle non-finite values.
Results may differ from the reference program's by a relative error of at most 0.008.
Values may be sent and summed in bfloat16 or wider, within the bound.
A program may use at most 64 MiB of HBM per device.

```python
import math
import jax
import jax.numpy as jnp
import numpy as np
from jax import lax

V = 256
PAIR_DEV = 2
RB = 2
NSH = 48
PAIRS = 256
BLOCKS = 128
ITEMS_DEV = 64
ITEMS = 32768
CAP_ITEMS = 2
REQ_DEV = 96
REQS = 12288
CAP_SHARE = 2
N_PAIRS = 128
N_INTS = 4


def draw_transpose_pair(key, part):
    half = PAIRS // (2 * PAIR_DEV)
    keys = jax.random.split(jax.random.fold_in(key, 7), half)
    perms = jax.vmap(lambda k: jax.random.permutation(k, PAIR_DEV))(keys).astype(jnp.int32)
    lower = (jnp.arange(half, dtype=jnp.int32)[:, None] + half) * PAIR_DEV + perms
    inverse = jnp.argsort(perms, axis=1).astype(jnp.int32)
    upper = jnp.arange(half, dtype=jnp.int32)[:, None] * PAIR_DEV + inverse
    return jnp.concatenate([lower.reshape(-1), upper.reshape(-1)])


def with_ends(drawn, own_key, low, high):
    spot = [jax.random.randint(jax.random.fold_in(own_key, axis), (), 0, length) for axis, length in enumerate(drawn.shape)]
    main_axis = drawn.shape.index(max(drawn.shape))
    beside = spot[:main_axis] + [(spot[main_axis] + 1) % drawn.shape[main_axis]] + spot[main_axis + 1:]
    return drawn.at[tuple(spot)].set(low).at[tuple(beside)].set(high)


def level_of(rng, extent, cuts, smallest, largest):
    gain = 1.0
    for position, blocks in cuts:
        steps = jax.random.uniform(jax.random.fold_in(jax.random.fold_in(rng, 6), position), (blocks,), jnp.float32, smallest / len(cuts), largest / len(cuts))
        gain = gain * jnp.repeat(jnp.exp(steps), extent[position] // blocks).reshape((-1,) + (1,) * (len(extent) - 1 - position))
    return gain


def routed_block(stream_key, own, number, rows, count, top, reach, lean):
    order = jax.random.permutation(stream_key, count)
    crowded, common = portions_of(count, rows * top, reach, lean, True), portions_of(count, rows * top, reach, lean, False)
    places = jnp.arange(count)

    def named(sizes, offset_by):
        used = int((sizes > 0).sum())
        fixed = max(1, used // 4)
        shifted = fixed + (places - fixed + offset_by * (used - fixed)) % max(1, count - fixed)
        return jnp.zeros((count,), jnp.int32).at[order[jnp.where(places < fixed, places, shifted)]].set(jnp.asarray(sizes, jnp.int32))

    sizes = jnp.where(number % 4 == 0, named(crowded, number // 4), named(common, number - number // 4 - 1))
    mixed = jax.random.permutation(jax.random.fold_in(own, 3), count)
    giver, sink = mixed[0:count // 2 * 2:2], mixed[1:count // 2 * 2:2]
    slack = jnp.minimum(sizes[giver] - 1, reach - sizes[sink]) // 2
    slack = jnp.where((giver == order[0]) | (sink == order[0]) | (sizes[sink] == 0), 0, jnp.maximum(slack, 0))
    shifted = jax.random.randint(jax.random.fold_in(own, 4), (count // 2,), 0, 1 << 20) % (slack + 1)
    sizes = sizes.at[giver].add(-shifted).at[sink].add(shifted)
    labels = jnp.searchsorted(jnp.cumsum(sizes), jnp.arange(rows * top), side="right").astype(jnp.int32)
    listing = labels.reshape(top, rows).T
    listing = listing[jax.random.permutation(jax.random.fold_in(own, 1), rows)]
    offset_by = jax.random.randint(jax.random.fold_in(own, 2), (rows, 1), 0, top)
    return jnp.take_along_axis(listing, (jnp.arange(top)[None, :] + offset_by) % top, axis=1)


def portions_of(amount, total, limit, lean, full):
    loads = [(1 << 20) // math.isqrt(standing ** lean) + 1 for standing in range(1, amount + 1)]
    largest = limit if full else min(limit, max(-(-total // amount), total * loads[0] // sum(loads)))
    least = 1 if total - largest >= amount - 1 else 0
    given, surplus = [largest] + [least] * (amount - 1), total - largest - least * (amount - 1)
    while surplus > 0:
        free = [i for i in range(1, amount) if given[i] < largest] or [i for i in range(1, amount) if given[i] < limit]
        whole, remaining = sum([loads[i] for i in free]), surplus
        for i in free:
            more = min(limit - given[i], max(1, remaining * loads[i] // whole), surplus)
            given[i] = given[i] + more
            surplus = surplus - more
    return np.array(given)


def bell_draw(stream_key, shape, spread, reach, cuts=(), kind=jnp.bfloat16):
    level = level_of(stream_key, shape, cuts, -0.22, 0.18) if cuts else 1.0
    drawn = jax.random.normal(stream_key, shape, jnp.float32) * spread * level
    return jnp.minimum(jnp.maximum(drawn, -reach), reach).astype(kind)


def setup_inputs(seed: int = 0) -> dict:
    splits = jax.random.split(jax.random.key(seed), 11)
    amps = bell_draw(splits[0], (PAIRS, V, V), 0.1, 0.8, ((0, 128), (1, 4)), jnp.float32)
    resid_rest = bell_draw(splits[1], (PAIRS, V, V), 1.0, 6.0, ((0, 128), (1, 4)), jnp.float32)
    int_blocks = bell_draw(splits[2], (BLOCKS, V, V), V ** -0.5, 0.375, ((0, 128),))
    virt_energy = jnp.clip(0.5 + 2.5 * jax.random.uniform(splits[3], (PAIRS, V), jnp.float32) ** level_of(splits[3], (PAIRS, V), ((0, 128),), -0.2, 0.2), 0.5, 3.0)
    pair_energy = jnp.clip(-2.0 + 1.5 * jax.random.uniform(splits[4], (PAIRS,), jnp.float32) ** level_of(splits[4], (PAIRS,), ((0, 128),), -0.2, 0.2), -2.0, -0.5)
    item_block_keys = jax.random.split(jax.random.fold_in(splits[5], 1), ITEMS // ITEMS_DEV)
    item_block_turns = jax.random.permutation(jax.random.fold_in(splits[5], 3), ITEMS // ITEMS_DEV)
    item_block = jax.vmap(lambda own, number: routed_block(jax.random.fold_in(splits[5], 2), own, number, ITEMS_DEV, N_PAIRS, 1, CAP_ITEMS, 2))(item_block_keys, item_block_turns).reshape((ITEMS, 1))
    share_owner_keys = jax.random.split(jax.random.fold_in(splits[6], 1), REQS // REQ_DEV)
    share_owner_turns = jax.random.permutation(jax.random.fold_in(splits[6], 3), REQS // REQ_DEV)
    share_owner = jax.vmap(lambda own, number: routed_block(jax.random.fold_in(splits[6], 2), own, number, REQ_DEV, N_PAIRS, 1, CAP_SHARE, 2))(share_owner_keys, share_owner_turns).reshape((REQS, 1))
    share_pair = with_ends(jax.random.randint(splits[7], (REQS, 1), 0, PAIR_DEV), jax.random.fold_in(splits[7], 1), 0, PAIR_DEV - 1).astype(jnp.int32)
    share_amp = with_ends(jax.random.randint(splits[8], (REQS, 1), 0, PAIR_DEV), jax.random.fold_in(splits[8], 1), 0, PAIR_DEV - 1).astype(jnp.int32)
    transpose_pair = draw_transpose_pair(jax.random.fold_in(splits[10], 71), 0)
    return dict(amps=amps, resid_rest=resid_rest, int_blocks=int_blocks, virt_energy=virt_energy, pair_energy=pair_energy, item_block=item_block, share_owner=share_owner, share_pair=share_pair, share_amp=share_amp, transpose_pair=transpose_pair)


def reference(amps, resid_rest, int_blocks, virt_energy, pair_energy, item_block, share_owner, share_pair, share_amp, transpose_pair):
    amp_half = amps.astype(jnp.bfloat16)
    row_blocks = V // RB
    sub_count = row_blocks // N_INTS
    block_ids = item_block[:, 0].reshape(N_PAIRS, N_INTS, PAIR_DEV, sub_count)
    block_ids = jnp.transpose(block_ids, (0, 2, 1, 3)).reshape(PAIRS, row_blocks)
    row_share = V // N_INTS

    def pair_terms(packed):
        amp_one, ids = packed
        pieces = amp_one.reshape(row_blocks, RB, V).astype(jnp.float32)
        chosen = int_blocks[ids].astype(jnp.float32)
        product = jnp.einsum("rik,rkj->rij", pieces, chosen).reshape(V, V).astype(jnp.bfloat16)
        left = amp_one.reshape(N_INTS, row_share, V).astype(jnp.float32)
        right = product.reshape(N_INTS, row_share, V).astype(jnp.float32)
        partials = jnp.einsum("qac,qad->qcd", left, right).astype(jnp.bfloat16)
        partials = lax.optimization_barrier(partials).astype(jnp.float32)
        return jnp.sum(partials, axis=0).astype(jnp.bfloat16)

    intermed = lax.map(pair_terms, (amp_half, block_ids))
    source = share_owner[:, 0].reshape(PAIRS, NSH) * PAIR_DEV + share_pair[:, 0].reshape(PAIRS, NSH)
    home = (jnp.arange(PAIRS, dtype=jnp.int32) // PAIR_DEV)[:, None] * PAIR_DEV + share_amp[:, 0].reshape(PAIRS, NSH)

    def cycle_one(packed):
        src, amp_index = packed
        return jnp.einsum("kac,kcb->ab", intermed[src].astype(jnp.float32), amp_half[amp_index].astype(jnp.float32))

    cycle_term = lax.map(cycle_one, (source, home))
    divisor = virt_energy[:, :, None] + virt_energy[:, None, :] - pair_energy[:, None, None]
    scaled = (resid_rest + cycle_term) / divisor
    return -0.5 * (scaled + jnp.transpose(scaled[transpose_pair], (0, 2, 1)))
```

```python
import functools

import jax
import jax.numpy as jnp
from jax import lax
from jax.experimental import pallas as pl
from jax.experimental.pallas import tpu as pltpu
from jax.sharding import Mesh
from jax.sharding import PartitionSpec as P

PAIRS = ("pairs_0", "pairs_1", "pairs_2")
PAIRS_INTS = ("pairs_0", "pairs_1", "pairs_2", "ints")
MESH = pl.DeviceIdType.MESH
F32 = jnp.float32
BF16 = jnp.bfloat16
NX, NZ, NC, NY = 4, 16, 2, 4
V = 256
SL = V // NY
ROWS = 2 * SL
HALF = SL // 2
CAP = 4
BLK8 = NX * NC
SLOTS = NY * BLK8 * CAP
UNITS = NZ * NC * 2
EB = 16


def iota(shape, dim):
    return lax.broadcasted_iota(jnp.int32, shape, dim)


def dot_nt(a, b):
    return lax.dot_general(a, b, (((1,), (1,)), ((), ())), preferred_element_type=F32)


def dot(a, b):
    return jnp.dot(a, b, preferred_element_type=F32)


def kernel(
    amps_ref,
    resid_ref,
    block_ref,
    ecol_ref,
    erow_ref,
    bcol_ref,
    brow_ref,
    unit_ref,
    mate_ref,
    swap_ref,
    out_ref,
    turned,
    blocks,
    amp_all,
    slot_all,
    counts,
    spread,
    slotted,
    inter_acc,
    inter,
    w_send,
    w_recv,
    scaled,
    m_send,
    m_recv,
    send_sem,
    y_recv,
    s_recv,
    n_recv,
    z_recv,
    xw_recv,
    xh_recv,
    core_recv,
    g_recv,
    gc_recv,
    w_rsem,
    m_rsem,
):
    x = lax.axis_index("pairs_0")
    z = lax.axis_index("pairs_1")
    c = lax.axis_index("pairs_2")
    y = lax.axis_index("ints")
    mate = {"pairs_2": 1 - c}
    x_up = {"pairs_0": lax.rem(x + 1, NX)}
    x_down = {"pairs_0": lax.rem(x + NX - 1, NX)}
    z_up = {"pairs_1": lax.rem(z + 1, NZ)}
    z_down = {"pairs_1": lax.rem(z + NZ - 1, NZ)}

    def at_xy(dx, dy):
        return {"pairs_0": lax.rem(x + dx, NX), "ints": lax.rem(y + dy, NY)}

    def remote(src, dst, ssem, rsem, device):
        return pltpu.make_async_remote_copy(
            src_ref=src, dst_ref=dst, send_sem=ssem, recv_sem=rsem, device_id=device, device_id_type=MESH
        )

    def await_bytes(ref, sem):
        pltpu.make_async_copy(ref, ref, sem).wait()

    barrier = pltpu.get_barrier_semaphore()
    offsets = [(dx, dy) for dx in range(NX) for dy in range(NY) if dx or dy]
    greeted = [z_up, z_down, mate] + [at_xy(dx, dy) for dx, dy in offsets]
    for device in greeted:
        pl.semaphore_signal(barrier, inc=1, device_id=device, device_id_type=MESH)

    turned[...] = jnp.transpose(block_ref[...].astype(F32))
    blocks[x, z, c] = turned[pl.ds(pl.multiple_of(y * SL, SL), SL), :].astype(BF16)
    amp_all[y] = amps_ref[...].astype(BF16)

    col = bcol_ref[...]
    row = brow_ref[...]
    earlier = (col == row) & (iota((ROWS, ROWS), 0) < iota((ROWS, ROWS), 1))
    rank = jnp.sum(earlier.astype(F32), axis=0, keepdims=True)
    z_of = (row >> 1) & (NZ - 1)
    place = z_of * (BLK8 * CAP) + ((row >> 5) * NC + (row & 1)) * CAP
    slot_all[y] = jnp.broadcast_to(place.astype(F32) + rank, (8, ROWS))

    n_req = unit_ref.shape[0]
    hot = (unit_ref[...] == iota((n_req, V), 1)).astype(F32).astype(BF16)
    out_id = iota((16, n_req), 0)
    mine = (iota((16, n_req), 1) // (n_req // 2)) * 2 + mate_ref[...]
    pick = (out_id == mine).astype(F32).astype(BF16)
    counts[x] = dot(pick, hot).astype(BF16)

    pl.semaphore_wait(barrier, len(greeted))

    def send_piece(ref, ssem, rsem, device):
        remote(ref, ref, ssem, rsem, device).start()

    def z_piece(zz, up, down):
        piece = blocks.at[x, zz, c]
        if up is not None:

            @pl.when(up)
            def _():
                send_piece(piece, send_sem.at[0], z_recv.at[zz], z_up)

        if down is not None:

            @pl.when(down)
            def _():
                send_piece(piece, send_sem.at[0], z_recv.at[zz], z_down)

        send_piece(piece, send_sem.at[1], xw_recv.at[0, zz], x_up)
        send_piece(piece, send_sem.at[1], xw_recv.at[1, zz], x_down)
        send_piece(piece, send_sem.at[2], core_recv.at[0], mate)

    z_piece(z, True, True)
    for dy in range(1, NY):
        send_piece(slot_all.at[y], send_sem.at[3], s_recv.at[dy], at_xy(0, dy))
        send_piece(amp_all.at[y], send_sem.at[4], y_recv.at[dy], at_xy(0, dy))
    for dx in range(1, NX):
        send_piece(counts.at[x], send_sem.at[5], n_recv.at[dx], at_xy(dx, 0))

    xl, xr, xo = lax.rem(x + NX - 1, NX), lax.rem(x + 1, NX), lax.rem(x + 2, NX)

    def x_piece(zz):
        await_bytes(blocks.at[xl, zz, c], xw_recv.at[0, zz])
        low = blocks.at[xl, zz, c, pl.ds(0, HALF), :]
        send_piece(low, send_sem.at[1], xh_recv.at[0, zz], x_up)
        send_piece(blocks.at[xl, zz, c], send_sem.at[2], core_recv.at[0], mate)
        await_bytes(blocks.at[xr, zz, c], xw_recv.at[1, zz])
        high = blocks.at[xr, zz, c, pl.ds(HALF, HALF), :]
        send_piece(high, send_sem.at[1], xh_recv.at[1, zz], x_down)
        send_piece(blocks.at[xr, zz, c], send_sem.at[2], core_recv.at[0], mate)

    def far_piece(zz):
        await_bytes(blocks.at[xo, zz, c, pl.ds(0, HALF), :], xh_recv.at[0, zz])
        await_bytes(blocks.at[xo, zz, c, pl.ds(HALF, HALF), :], xh_recv.at[1, zz])
        send_piece(blocks.at[xo, zz, c], send_sem.at[2], core_recv.at[0], mate)

    last = NZ // 2

    def both(s, work):
        @pl.when((s >= 0) & (s <= last))
        def _():
            work(lax.rem(z - s + NZ, NZ))

        @pl.when((s >= 1) & (s < last))
        def _():
            work(lax.rem(z + s, NZ))

    def gather_step(s, carry):
        @pl.when(s <= last)
        def _():
            zz = lax.rem(z - s + NZ, NZ)
            await_bytes(blocks.at[x, zz, c], z_recv.at[zz])
            z_piece(zz, s < last, None)

        @pl.when(s < last)
        def _():
            zz = lax.rem(z + s, NZ)
            await_bytes(blocks.at[x, zz, c], z_recv.at[zz])
            z_piece(zz, None, s < last - 1)

        both(s - 1, x_piece)
        both(s - 2, far_piece)
        return carry

    lax.fori_loop(1, last + 3, gather_step, 0)

    for dy in range(1, NY):
        other = lax.rem(y + NY - dy, NY)
        await_bytes(slot_all.at[other], s_recv.at[dy])
        await_bytes(amp_all.at[other], y_recv.at[dy])
    group = BLK8 * CAP
    for q in range(NY):
        slot_of = slot_all[q, 0:1, :]
        here = slot_of == iota((NZ * group, ROWS), 0).astype(F32)
        lane = iota((NZ * group, ROWS), 1)
        rows = amp_all[q]
        for p in range(2):
            own = here & ((lane >= SL) if p else (lane < SL))
            part = dot(own.astype(F32).astype(BF16), rows).astype(BF16)
            slotted[:, pl.ds(q * group, group), pl.ds(p * V, V)] = part.reshape(NZ, group, V)

    for dx in range(1, NX):
        await_bytes(counts.at[lax.rem(x + NX - dx, NX)], n_recv.at[dx])
    n_out = NX * 4
    tall = iota((n_out * EB, NX * 16), 0) // EB
    pick_row = (iota((n_out * EB, NX * 16), 1) == (tall // 4) * 16 + lax.rem(tall, 4)).astype(F32).astype(BF16)
    tall_counts = dot(pick_row, counts[...].reshape(NX * 16, V)).astype(BF16)
    wide = iota((V, UNITS * EB), 1) // EB + x * UNITS
    pick_col = (iota((V, UNITS * EB), 0) == wide).astype(F32).astype(BF16)
    full = dot(tall_counts, pick_col)
    same = lax.rem(iota(full.shape, 0), EB) == lax.rem(iota(full.shape, 1), EB)
    spread[...] = jnp.where(same, full, 0.0).astype(BF16)

    await_bytes(blocks.at[:, :, 1 - c], core_recv.at[0])

    inter_acc[...] = jnp.zeros_like(inter_acc)
    lane_block = lax.rem(iota((SL, SLOTS), 1), group) // CAP

    def block_step(zz, carry):
        rows = slotted[zz]
        both_rows = rows[:, :V] + rows[:, V:]
        all_b = jnp.concatenate([blocks[k // NC, zz, k % NC] for k in range(BLK8)], axis=0)
        raw = dot_nt(all_b, both_rows)
        prod = jnp.zeros((SL, SLOTS), F32)
        for k in range(BLK8):
            prod = jnp.where(lane_block == k, raw[k * SL : (k + 1) * SL], prod)
        inter_acc[...] += dot(prod.astype(BF16), rows)
        return carry

    lax.fori_loop(0, NZ, block_step, 0)

    for p in range(2):
        inter[z, c, p] = inter_acc[:, pl.ds(p * V, V)].astype(BF16)

    def g_piece(zz, p, up, down):
        piece = inter.at[zz, c, p]
        if up is not None:

            @pl.when(up)
            def _():
                send_piece(piece, send_sem.at[6], g_recv.at[zz, p], z_up)

        if down is not None:

            @pl.when(down)
            def _():
                send_piece(piece, send_sem.at[6], g_recv.at[zz, p], z_down)

        send_piece(piece, send_sem.at[7], gc_recv.at[0], mate)

    for p in range(2):
        g_piece(z, p, True, True)

    def ring_step(s, carry):
        for p in range(2):
            zz = lax.rem(z - s + NZ, NZ)
            await_bytes(inter.at[zz, c, p], g_recv.at[zz, p])
            g_piece(zz, p, s < last, None)

            @pl.when(s < last)
            def _():
                zl = lax.rem(z + s, NZ)
                await_bytes(inter.at[zl, c, p], g_recv.at[zl, p])
                g_piece(zl, p, None, s < last - 1)

        return carry

    lax.fori_loop(1, last + 1, ring_step, 0)
    await_bytes(inter.at[:, 1 - c], gc_recv.at[0])

    low_lane = iota((EB, 128), 1) < SL

    def sum_step(eb, carry):
        at = pl.ds(pl.multiple_of(eb * EB, EB), EB)
        part = inter[:, :, :, at, :].reshape(UNITS * EB, V)
        sums = dot(spread[...], part)
        for xd in range(NX):
            for p in range(2):
                base = (xd * 4 + p * 2) * EB
                first, second = sums[base : base + EB], sums[base + EB : base + 2 * EB]
                for yd in range(NY):
                    t = (yd // 2) * 128
                    f, g = first[:, t : t + 128], second[:, t : t + 128]
                    if yd % 2 == 0:
                        joined = jnp.where(low_lane, f, pltpu.roll(g, SL, 1))
                    else:
                        joined = jnp.where(low_lane, pltpu.roll(f, SL, 1), g)
                    w_send[xd, yd, p, at, :] = joined.astype(BF16)
        return carry

    lax.fori_loop(0, SL // EB, sum_step, 0)

    for dx, dy in offsets:
        there = at_xy(dx, dy)
        remote(
            w_send.at[there["pairs_0"], there["ints"]],
            w_recv.at[dx, dy],
            send_sem.at[8 if dx else 10],
            w_rsem.at[dx, dy],
            there,
        ).start()
    w_recv[0, 0] = w_send[x, y]
    for dx, dy in offsets:
        await_bytes(w_recv.at[dx, dy], w_rsem.at[dx, dy])

    lane_low = iota((SL, 128), 1) < SL
    for p in range(2):
        parts = []
        for q in range(NY):
            dy = lax.rem(y - q + NY, NY)
            parts.append(sum(w_recv[dx, dy, p].astype(F32) for dx in range(NX)))
        w = jnp.transpose(jnp.concatenate(parts, axis=0)).astype(BF16)
        cycle = jnp.zeros((SL, V), F32)
        for j in range(2):
            rows = amp_all[:, pl.ds(j * SL, SL), :].reshape(V, V)
            cycle += dot(w[j * SL : (j + 1) * SL], rows)
        mine_rows = ecol_ref[p, pl.ds(pl.multiple_of(y * SL, SL), SL), :]
        scaled[p] = (resid_ref[p] + cycle) / (mine_rows + erow_ref[p])
    for q in range(NY):
        t = (q // 2) * 128
        f, g = scaled[0, :, pl.ds(t, 128)], scaled[1, :, pl.ds(t, 128)]
        if q % 2 == 0:
            joined = jnp.where(lane_low, f, pltpu.roll(g, SL, 1))
        else:
            joined = jnp.where(lane_low, pltpu.roll(f, SL, 1), g)
        m_send[q] = joined.astype(BF16)
    for dy in range(NY):
        there = at_xy(NX // 2, dy)
        remote(m_send.at[there["ints"]], m_recv.at[dy], send_sem.at[9], m_rsem.at[dy], there).start()
    for dy in range(NY):
        await_bytes(m_recv.at[dy], m_rsem.at[dy])
    mirror = jnp.concatenate([m_recv[lax.rem(y - q + NY, NY)].astype(F32) for q in range(NY)], axis=0)
    mirror = jnp.transpose(mirror)
    for p in range(2):
        other = jnp.where(swap_ref[p] > 0.5, mirror[SL:], mirror[:SL])
        out_ref[p] = -0.5 * (scaled[p] + other)

    await_bytes(blocks.at[0, pl.ds(0, NZ - 1), 0], send_sem.at[0])
    await_bytes(blocks.at[pl.ds(0, NX - 1), :, 0], send_sem.at[1])
    await_bytes(blocks.at[:, :, 0], send_sem.at[2])
    await_bytes(slot_all.at[pl.ds(0, NY - 1)], send_sem.at[3])
    await_bytes(amp_all.at[pl.ds(0, NY - 1)], send_sem.at[4])
    await_bytes(counts.at[pl.ds(0, NX - 1)], send_sem.at[5])
    await_bytes(inter.at[pl.ds(0, NZ - 1), 0], send_sem.at[6])
    await_bytes(inter.at[:, 0], send_sem.at[7])
    await_bytes(w_recv.at[pl.ds(0, NX - 1)], send_sem.at[8])
    await_bytes(w_recv.at[0, pl.ds(0, NY - 1)], send_sem.at[10])
    await_bytes(m_recv.at[:], send_sem.at[9])


def body(
    amps,
    resid_rest,
    int_blocks,
    virt_energy,
    pair_energy,
    item_block,
    share_owner,
    share_pair,
    share_amp,
    transpose_pair,
):
    n_pairs = lax.axis_size(PAIRS)
    pair_index = lax.axis_index(PAIRS)
    partner = (pair_index + n_pairs // 2) % n_pairs
    swap = (transpose_pair - partner * 2).astype(F32).reshape(2, 1, 1)
    row_block = jnp.repeat(item_block[:, 0], 2)
    unit = share_owner * 2 + share_pair
    rows_energy = (virt_energy - pair_energy[:, None])[:, :, None]
    vmem = pl.BlockSpec(memory_space=pltpu.VMEM)
    dma = pltpu.SemaphoreType.DMA
    return pl.pallas_call(
        kernel,
        out_shape=jax.ShapeDtypeStruct((2, SL, V), F32),
        in_specs=[vmem] * 10,
        out_specs=vmem,
        scratch_shapes=[
            pltpu.VMEM((V, V), F32),
            pltpu.VMEM((NX, NZ, NC, SL, V), BF16),
            pltpu.VMEM((NY, ROWS, V), BF16),
            pltpu.VMEM((NY, 8, ROWS), F32),
            pltpu.VMEM((NX, 16, V), BF16),
            pltpu.VMEM((NX * 4 * EB, UNITS * EB), BF16),
            pltpu.VMEM((NZ, SLOTS, 2 * V), BF16),
            pltpu.VMEM((SL, 2 * V), F32),
            pltpu.VMEM((NZ, NC, 2, SL, V), BF16),
            pltpu.VMEM((NX, NY, 2, SL, 128), BF16),
            pltpu.VMEM((NX, NY, 2, SL, 128), BF16),
            pltpu.VMEM((2, SL, V), F32),
            pltpu.VMEM((NY, SL, 128), BF16),
            pltpu.VMEM((NY, SL, 128), BF16),
            dma((11,)),
            dma((NY,)),
            dma((NY,)),
            dma((NX,)),
            dma((NZ,)),
            dma((2, NZ)),
            dma((2, NZ)),
            dma((1,)),
            dma((NZ, 2)),
            dma((1,)),
            dma((NX, NY)),
            dma((NY,)),
        ],
        compiler_params=pltpu.CompilerParams(collective_id=0, has_side_effects=True),
        name="cycle",
    )(
        amps.reshape(ROWS, V),
        resid_rest,
        int_blocks[0],
        rows_energy,
        virt_energy[:, None, :],
        row_block[:, None],
        row_block[None, :],
        unit,
        share_amp.reshape(1, -1),
        swap,
    )


def solution(mesh):
    torus = Mesh(
        mesh.devices.reshape(NX, NZ, NC, mesh.shape["ints"]),
        ("pairs_0", "pairs_1", "pairs_2", "ints"),
    )
    return jax.shard_map(
        body,
        mesh=torus,
        in_specs=(
            P(PAIRS, "ints", None),
            P(PAIRS, "ints", None),
            P(PAIRS, None, None),
            P(PAIRS, None),
            P(PAIRS),
            P(PAIRS_INTS, None),
            P(PAIRS, None),
            P(PAIRS, None),
            P(PAIRS, None),
            P(PAIRS),
        ),
        out_specs=P(PAIRS, "ints", None),
        check_vma=False,
    )
```

```python
import functools

import jax
import jax.numpy as jnp
from jax import lax
from jax.experimental import pallas as pl
from jax.experimental.pallas import tpu as pltpu
from jax.sharding import Mesh
from jax.sharding import PartitionSpec as P

PAIRS = ("pairs_0", "pairs_1", "pairs_2")
PAIRS_INTS = ("pairs_0", "pairs_1", "pairs_2", "ints")
MESH = pl.DeviceIdType.MESH
F32 = jnp.float32
BF16 = jnp.bfloat16
NX, NZ, NC, NY = 4, 16, 2, 4
V = 256
SL = V // NY
ROWS = 2 * SL
HALF = SL // 2
CAP = 4
BLK8 = NX * NC
SLOTS = NY * BLK8 * CAP
UNITS = NZ * NC * 2
EB = 16
N_EB = SL // EB
BLOCK_PLAN = {0: (4, 2, 1), 2: (1,), 4: (4, 2, 1), 6: (1,)}
BLOCK_TIME = {1: 3.5, 2: 4.5, 4: 5.5, 3: 8.0, 5: 10.0, 6: 11.0, 7: 14.0, 8: 15.0}
RING_PLAN = {0: (4, 1), 1: (1,), 2: (1,), 4: (1,), 5: (1,), 6: (1,), 7: (1,)}
RING_TIME = {1: 2.4, 4: 4.2, 2: 4.8, 5: 6.6, 3: 7.2, 6: 9.0, 7: 11.4, 8: 13.8}


def sends_of(plan, offset):
    half = NZ // 2
    up = [k for k in plan.get(offset, ()) if offset >= 0 and offset + k <= half]
    down = [-k for k in plan.get(-offset, ()) if offset <= 0 and k - offset < half]
    return [k for pair in zip(up, down) for k in pair] if offset == 0 else up + down


def gather_events():
    pieces = [(0.0, 0)] + [(t, o) for o, t in BLOCK_TIME.items()] + [(t, -o) for o, t in BLOCK_TIME.items() if o < NZ // 2]
    pieces.sort()
    events = [(6.0, 5, 0, "slots"), (7.0, 5, 0, "spread")]
    near = far = 0.0
    for t, o in pieces:
        near = max(near + 0.9, t + 2.8)
        far = max(far + 1.0, near + 2.8)
        if o:
            events.append((t, 0, o, "z"))
        events += [(near, 1, o, "x"), (far, 2, o, "far"), (far + 2.0, 3, o, "work")]
    return [(kind, o) for _, _, o, kind in sorted(events)]


def iota(shape, dim):
    return lax.broadcasted_iota(jnp.int32, shape, dim)


def dot_nt(a, b):
    return lax.dot_general(a, b, (((1,), (1,)), ((), ())), preferred_element_type=F32)


def dot(a, b):
    return jnp.dot(a, b, preferred_element_type=F32)


def ring_events():
    events = []
    for eb in range(N_EB):
        events.append((1.5 * eb, eb, 0, "ring"))
        for o, t in RING_TIME.items():
            for signed in (o, -o) if o < NZ // 2 else (o,):
                events.append((t + eb + 1.0, eb, signed, "ring"))
        events.append((RING_TIME[NZ // 2] + eb + 3.0, eb, 0, "sum"))
    return [(kind, o, eb) for _, eb, o, kind in sorted(events)]


def kernel(
    amps_hbm,
    resid_hbm,
    block_hbm,
    energy_hbm,
    item_hbm,
    owner_hbm,
    pair_hbm,
    mate_hbm,
    pair_energy_hbm,
    twin_hbm,
    out_ref,
    turned,
    blocks,
    amp_all,
    slot_all,
    counts,
    spread,
    slotted,
    inter_acc,
    inter,
    w_send,
    w_recv,
    scaled,
    m_send,
    m_recv,
    ecol,
    amps_ref,
    resid,
    block_ref,
    energy_ref,
    item_ref,
    owner_ref,
    pair_ref,
    mate_ref,
    pair_energy_ref,
    twin_ref,
    local_sem,
    send_sem,
    y_recv,
    s_recv,
    n_recv,
    z_recv,
    xw_recv,
    xh_recv,
    core_recv,
    g_recv,
    gc_recv,
    w_rsem,
    m_rsem,
):
    x = lax.axis_index("pairs_0")
    z = lax.axis_index("pairs_1")
    c = lax.axis_index("pairs_2")
    y = lax.axis_index("ints")
    mate = {"pairs_2": 1 - c}
    x_up = {"pairs_0": lax.rem(x + 1, NX)}
    x_down = {"pairs_0": lax.rem(x + NX - 1, NX)}

    def at_z(k):
        return {"pairs_1": lax.rem(z + k + NZ, NZ)}

    def at_xy(dx, dy):
        return {"pairs_0": lax.rem(x + dx, NX), "ints": lax.rem(y + dy, NY)}

    def remote(src, dst, ssem, rsem, device):
        return pltpu.make_async_remote_copy(
            src_ref=src, dst_ref=dst, send_sem=ssem, recv_sem=rsem, device_id=device, device_id_type=MESH
        )

    def await_bytes(ref, sem):
        pltpu.make_async_copy(ref, ref, sem).wait()

    held = (amps_hbm, resid_hbm, block_hbm, energy_hbm, item_hbm, owner_hbm, pair_hbm, mate_hbm, pair_energy_hbm, twin_hbm)
    used = (amps_ref, resid, block_ref, energy_ref, item_ref, owner_ref, pair_ref, mate_ref, pair_energy_ref, twin_ref)
    copies = [pltpu.make_async_copy(a, b, local_sem.at[i]) for i, (a, b) in enumerate(zip(held, used))]
    for i in (2, 0, 4, 5, 6, 7, 3, 8, 9, 1):
        copies[i].start()

    barrier = pltpu.get_barrier_semaphore()
    offsets = [(dx, dy) for dx in range(NX) for dy in range(NY) if dx or dy]
    z_steps = sorted({k for plan in (BLOCK_PLAN, RING_PLAN) for steps in plan.values() for k in steps})
    greeted = [at_z(k) for step in z_steps for k in (step, -step)] + [mate] + [at_xy(dx, dy) for dx, dy in offsets]
    for device in greeted:
        pl.semaphore_signal(barrier, inc=1, device_id=device, device_id_type=MESH)

    copies[2].wait()
    turned[...] = jnp.transpose(block_ref[...].astype(F32))
    blocks[x, z, c] = turned[pl.ds(pl.multiple_of(y * SL, SL), SL), :].astype(BF16)
    copies[0].wait()
    amp_all[y] = amps_ref[...].astype(BF16)

    copies[4].wait()
    n_items = item_ref.shape[1]
    twice = (iota((n_items, ROWS), 0) == iota((n_items, ROWS), 1) // 2).astype(F32).astype(BF16)
    item = jnp.broadcast_to(item_ref[...].astype(F32), (16, n_items)).astype(BF16)
    row = dot(item, twice)[0:1].astype(jnp.int32)
    square = jnp.broadcast_to(row, (ROWS, ROWS)).astype(F32)
    earlier = (jnp.transpose(square) == square) & (iota((ROWS, ROWS), 0) < iota((ROWS, ROWS), 1))
    rank = jnp.sum(earlier.astype(F32), axis=0, keepdims=True)
    z_of = (row >> 1) & (NZ - 1)
    place = z_of * (BLK8 * CAP) + ((row >> 5) * NC + (row & 1)) * CAP
    slot_all[y] = jnp.broadcast_to(place.astype(F32) + rank, (8, ROWS))

    for i in (5, 6, 7):
        copies[i].wait()
    n_req = owner_ref.shape[1]
    unit = owner_ref[...] * 2 + pair_ref[...]
    hot = (iota((V, n_req), 0) == unit).astype(F32).astype(BF16)
    out_id = iota((16, n_req), 0)
    mine = (iota((16, n_req), 1) // (n_req // 2)) * 2 + mate_ref[...]
    pick = (out_id == mine).astype(F32).astype(BF16)
    counts[x] = dot_nt(pick, hot).astype(BF16)

    pl.semaphore_wait(barrier, len(greeted))

    def send_piece(ref, ssem, rsem, device):
        remote(ref, ref, ssem, rsem, device).start()

    def z_of_piece(o):
        return lax.rem(z - o + NZ, NZ)

    def z_piece(o):
        zz = z_of_piece(o)
        piece = blocks.at[x, zz, c]
        if o:
            await_bytes(piece, z_recv.at[zz])
        for k in sends_of(BLOCK_PLAN, o):
            send_piece(piece, send_sem.at[0], z_recv.at[zz], at_z(k))
        send_piece(piece, send_sem.at[1], xw_recv.at[0, zz], x_up)
        send_piece(piece, send_sem.at[1], xw_recv.at[1, zz], x_down)
        send_piece(piece, send_sem.at[2], core_recv.at[zz], mate)

    xl, xr, xo = lax.rem(x + NX - 1, NX), lax.rem(x + 1, NX), lax.rem(x + 2, NX)

    def x_piece(o):
        zz = z_of_piece(o)
        await_bytes(blocks.at[xl, zz, c], xw_recv.at[0, zz])
        low = blocks.at[xl, zz, c, pl.ds(0, HALF), :]
        send_piece(low, send_sem.at[1], xh_recv.at[0, zz], x_up)
        send_piece(blocks.at[xl, zz, c], send_sem.at[2], core_recv.at[zz], mate)
        await_bytes(blocks.at[xr, zz, c], xw_recv.at[1, zz])
        high = blocks.at[xr, zz, c, pl.ds(HALF, HALF), :]
        send_piece(high, send_sem.at[1], xh_recv.at[1, zz], x_down)
        send_piece(blocks.at[xr, zz, c], send_sem.at[2], core_recv.at[zz], mate)

    def far_piece(o):
        zz = z_of_piece(o)
        await_bytes(blocks.at[xo, zz, c, pl.ds(0, HALF), :], xh_recv.at[0, zz])
        await_bytes(blocks.at[xo, zz, c, pl.ds(HALF, HALF), :], xh_recv.at[1, zz])
        send_piece(blocks.at[xo, zz, c], send_sem.at[2], core_recv.at[zz], mate)

    group = BLK8 * CAP

    def slot_rows():
        for dy in range(1, NY):
            other = lax.rem(y + NY - dy, NY)
            await_bytes(slot_all.at[other], s_recv.at[dy])
            await_bytes(amp_all.at[other], y_recv.at[dy])
        for q in range(NY):
            slot_of = slot_all[q, 0:1, :]
            here = slot_of == iota((NZ * group, ROWS), 0).astype(F32)
            lane = iota((NZ * group, ROWS), 1)
            rows = amp_all[q]
            for p in range(2):
                own = here & ((lane >= SL) if p else (lane < SL))
                part = dot(own.astype(F32).astype(BF16), rows).astype(BF16)
                slotted[:, pl.ds(q * group, group), pl.ds(p * V, V)] = part.reshape(NZ, group, V)

    def spread_counts():
        for dx in range(1, NX):
            await_bytes(counts.at[lax.rem(x + NX - dx, NX)], n_recv.at[dx])
        n_out = NX * 4
        tall = iota((n_out * EB, NX * 16), 0) // EB
        pick_row = (iota((n_out * EB, NX * 16), 1) == (tall // 4) * 16 + lax.rem(tall, 4)).astype(F32).astype(BF16)
        tall_counts = dot(pick_row, counts[...].reshape(NX * 16, V)).astype(BF16)
        wide = iota((V, UNITS * EB), 1) // EB + x * UNITS
        pick_col = (iota((V, UNITS * EB), 0) == wide).astype(F32).astype(BF16)
        full = dot(tall_counts, pick_col)
        same = lax.rem(iota(full.shape, 0), EB) == lax.rem(iota(full.shape, 1), EB)
        spread[...] = jnp.where(same, full, 0.0).astype(BF16)
        copies[3].wait()
        for p in range(2):
            ecol[p] = jnp.transpose(jnp.broadcast_to(energy_ref[p : p + 1, :], (128, V)))

    lane_block = lax.rem(iota((SL, SLOTS), 1), group) // CAP

    def block_work(o):
        zz = z_of_piece(o)
        await_bytes(blocks.at[:, zz, 1 - c], core_recv.at[zz])
        rows = slotted[zz]
        both_rows = rows[:, :V] + rows[:, V:]
        all_b = jnp.concatenate([blocks[k // NC, zz, k % NC] for k in range(BLK8)], axis=0)
        raw = dot_nt(all_b, both_rows)
        prod = jnp.zeros((SL, SLOTS), F32)
        for k in range(BLK8):
            prod = jnp.where(lane_block == k, raw[k * SL : (k + 1) * SL], prod)
        inter_acc[...] += dot(prod.astype(BF16), rows)

    z_piece(0)
    for dy in range(1, NY):
        send_piece(slot_all.at[y], send_sem.at[3], s_recv.at[dy], at_xy(0, dy))
        send_piece(amp_all.at[y], send_sem.at[4], y_recv.at[dy], at_xy(0, dy))
    for dx in range(1, NX):
        send_piece(counts.at[x], send_sem.at[5], n_recv.at[dx], at_xy(dx, 0))
    inter_acc[...] = jnp.zeros_like(inter_acc)

    for kind, o in gather_events():
        if kind == "slots":
            slot_rows()
        elif kind == "spread":
            spread_counts()
        else:
            {"z": z_piece, "x": x_piece, "far": far_piece, "work": block_work}[kind](o)

    for eb in range(N_EB):
        for p in range(2):
            inter[eb, z, c, p] = inter_acc[pl.ds(eb * EB, EB), pl.ds(p * V, V)].astype(BF16)

    def ring_piece(o, eb):
        zz = z_of_piece(o)
        piece = inter.at[eb, zz, c]
        if o:
            await_bytes(piece, g_recv.at[eb, zz])
        for k in sends_of(RING_PLAN, o):
            send_piece(piece, send_sem.at[6], g_recv.at[eb, zz], at_z(k))
        send_piece(piece, send_sem.at[7], gc_recv.at[eb], mate)

    low_lane = iota((EB, 128), 1) < SL

    def sum_part(eb):
        await_bytes(inter.at[eb, :, 1 - c], gc_recv.at[eb])
        part = inter[eb].reshape(UNITS * EB, V)
        sums = dot(spread[...], part)
        for xd in range(NX):
            for p in range(2):
                base = (xd * 4 + p * 2) * EB
                first, second = sums[base : base + EB], sums[base + EB : base + 2 * EB]
                for yd in range(NY):
                    t = (yd // 2) * 128
                    f, g = first[:, t : t + 128], second[:, t : t + 128]
                    if yd % 2 == 0:
                        joined = jnp.where(low_lane, f, pltpu.roll(g, SL, 1))
                    else:
                        joined = jnp.where(low_lane, pltpu.roll(f, SL, 1), g)
                    w_send[xd, yd, eb, p] = joined.astype(BF16)
        for dx, dy in offsets:
            there = at_xy(dx, dy)
            remote(
                w_send.at[there["pairs_0"], there["ints"], eb],
                w_recv.at[dx, dy, eb],
                send_sem.at[8 if dx else 10],
                w_rsem.at[dx, dy],
                there,
            ).start()

    for kind, o, eb in ring_events():
        if kind == "ring":
            ring_piece(o, eb)
        else:
            sum_part(eb)

    w_recv[0, 0] = w_send[x, y]
    for i in (1, 8, 9):
        copies[i].wait()
    for dx, dy in offsets:
        await_bytes(w_recv.at[dx, dy], w_rsem.at[dx, dy])

    lane_low = iota((SL, 128), 1) < SL
    for p in range(2):
        parts = []
        for q in range(NY):
            dy = lax.rem(y - q + NY, NY)
            for eb in range(N_EB):
                parts.append(sum(w_recv[dx, dy, eb, p].astype(F32) for dx in range(NX)))
        w = jnp.transpose(jnp.concatenate(parts, axis=0)).astype(BF16)
        cycle = jnp.zeros((SL, V), F32)
        for j in range(2):
            rows = amp_all[:, pl.ds(j * SL, SL), :].reshape(V, V)
            cycle += dot(w[j * SL : (j + 1) * SL], rows)
        mine_rows = ecol[p, pl.ds(pl.multiple_of(y * SL, SL), SL), :]
        mine_rows = jnp.concatenate([mine_rows, mine_rows], axis=1)
        divisor = mine_rows + energy_ref[p : p + 1, :] - pair_energy_ref[p]
        scaled[p] = (resid[p] + cycle) / divisor
    for q in range(NY):
        t = (q // 2) * 128
        f, g = scaled[0, :, pl.ds(t, 128)], scaled[1, :, pl.ds(t, 128)]
        if q % 2 == 0:
            joined = jnp.where(lane_low, f, pltpu.roll(g, SL, 1))
        else:
            joined = jnp.where(lane_low, pltpu.roll(f, SL, 1), g)
        m_send[q] = joined.astype(BF16)
    for dy in range(NY):
        there = at_xy(NX // 2, dy)
        remote(m_send.at[there["ints"]], m_recv.at[dy], send_sem.at[9], m_rsem.at[dy], there).start()
    for dy in range(NY):
        await_bytes(m_recv.at[dy], m_rsem.at[dy])
    mirror = jnp.concatenate([m_recv[lax.rem(y - q + NY, NY)].astype(F32) for q in range(NY)], axis=0)
    mirror = jnp.transpose(mirror)
    first_twin = ((xo * NZ + z) * NC + c) * 2
    for p in range(2):
        which = jnp.full((SL, V), twin_ref[p] - first_twin)
        other = jnp.where(which == 1, mirror[SL:], mirror[:SL])
        out_ref[p] = -0.5 * (scaled[p] + other)

    await_bytes(blocks.at[0, pl.ds(0, NZ - 1), 0], send_sem.at[0])
    await_bytes(blocks.at[pl.ds(0, NX - 1), :, 0], send_sem.at[1])
    await_bytes(blocks.at[:, :, 0], send_sem.at[2])
    await_bytes(slot_all.at[pl.ds(0, NY - 1)], send_sem.at[3])
    await_bytes(amp_all.at[pl.ds(0, NY - 1)], send_sem.at[4])
    await_bytes(counts.at[pl.ds(0, NX - 1)], send_sem.at[5])
    await_bytes(inter.at[:, pl.ds(0, NZ - 1), 0], send_sem.at[6])
    await_bytes(inter.at[:, :, 0], send_sem.at[7])
    await_bytes(w_recv.at[pl.ds(0, NX - 1)], send_sem.at[8])
    await_bytes(w_recv.at[0, pl.ds(0, NY - 1)], send_sem.at[10])
    await_bytes(m_recv.at[:], send_sem.at[9])


def body(
    amps,
    resid_rest,
    int_blocks,
    virt_energy,
    pair_energy,
    item_block,
    share_owner,
    share_pair,
    share_amp,
    transpose_pair,
):
    n_items, n_req = item_block.shape[0], share_owner.shape[0]
    dma = pltpu.SemaphoreType.DMA
    return pl.pallas_call(
        kernel,
        out_shape=jax.ShapeDtypeStruct((2, SL, V), F32),
        in_specs=[pl.BlockSpec(memory_space=pl.ANY)] * 10,
        out_specs=pl.BlockSpec(memory_space=pltpu.VMEM),
        scratch_shapes=[
            pltpu.VMEM((V, V), F32),
            pltpu.VMEM((NX, NZ, NC, SL, V), BF16),
            pltpu.VMEM((NY, ROWS, V), BF16),
            pltpu.VMEM((NY, 8, ROWS), F32),
            pltpu.VMEM((NX, 16, V), BF16),
            pltpu.VMEM((NX * 4 * EB, UNITS * EB), BF16),
            pltpu.VMEM((NZ, SLOTS, 2 * V), BF16),
            pltpu.VMEM((SL, 2 * V), F32),
            pltpu.VMEM((N_EB, NZ, NC, 2, EB, V), BF16),
            pltpu.VMEM((NX, NY, N_EB, 2, EB, 128), BF16),
            pltpu.VMEM((NX, NY, N_EB, 2, EB, 128), BF16),
            pltpu.VMEM((2, SL, V), F32),
            pltpu.VMEM((NY, SL, 128), BF16),
            pltpu.VMEM((NY, SL, 128), BF16),
            pltpu.VMEM((2, V, 128), F32),
            pltpu.VMEM((ROWS, V), F32),
            pltpu.VMEM((2, SL, V), F32),
            pltpu.VMEM((V, V), BF16),
            pltpu.VMEM((2, V), F32),
            pltpu.VMEM((1, n_items), jnp.int32),
            pltpu.VMEM((1, n_req), jnp.int32),
            pltpu.VMEM((1, n_req), jnp.int32),
            pltpu.VMEM((1, n_req), jnp.int32),
            pltpu.SMEM((2,), F32),
            pltpu.SMEM((2,), jnp.int32),
            dma((10,)),
            dma((11,)),
            dma((NY,)),
            dma((NY,)),
            dma((NX,)),
            dma((NZ,)),
            dma((2, NZ)),
            dma((2, NZ)),
            dma((NZ,)),
            dma((N_EB, NZ)),
            dma((N_EB,)),
            dma((NX, NY)),
            dma((NY,)),
        ],
        compiler_params=pltpu.CompilerParams(collective_id=0, has_side_effects=True),
        name="cycle",
    )(
        amps.reshape(ROWS, V),
        resid_rest,
        int_blocks[0],
        virt_energy,
        item_block.reshape(1, -1),
        share_owner.reshape(1, -1),
        share_pair.reshape(1, -1),
        share_amp.reshape(1, -1),
        pair_energy,
        transpose_pair,
    )


def solution(mesh):
    torus = Mesh(
        mesh.devices.reshape(NX, NZ, NC, mesh.shape["ints"]),
        ("pairs_0", "pairs_1", "pairs_2", "ints"),
    )
    return jax.shard_map(
        body,
        mesh=torus,
        in_specs=(
            P(PAIRS, "ints", None),
            P(PAIRS, "ints", None),
            P(PAIRS, None, None),
            P(PAIRS, None),
            P(PAIRS),
            P(PAIRS_INTS, None),
            P(PAIRS, None),
            P(PAIRS, None),
            P(PAIRS, None),
            P(PAIRS),
        ),
        out_specs=P(PAIRS, "ints", None),
        check_vma=False,
    )
```

```python
import functools

import jax
import jax.numpy as jnp
from jax import lax
from jax.experimental import pallas as pl
from jax.experimental.pallas import tpu as pltpu
from jax.sharding import Mesh
from jax.sharding import PartitionSpec as P

PAIRS = ("pairs_0", "pairs_1", "pairs_2")
PAIRS_INTS = ("pairs_0", "pairs_1", "pairs_2", "ints")
MESH = pl.DeviceIdType.MESH
F32 = jnp.float32
BF16 = jnp.bfloat16
NX, NZ, NC, NY = 4, 16, 2, 4
V = 256
SL = V // NY
ROWS = 2 * SL
HALF = SL // 2
CAP = 4
BLK8 = NX * NC
SLOTS = NY * BLK8 * CAP
UNITS = NZ * NC * 2
EB = 16
N_EB = SL // EB
FIRST = 16
REST = SL - FIRST
BLOCK_PLAN = {0: (1, 3), 1: (1,), 3: (1, 3), 4: (1,), 6: (1, 2)}
FIRST_PLAN = {0: (1,), 1: (3, 1), 2: (1,), 3: (2,), 4: (2,), 6: (2, 1)}
RING_PLAN = {0: (3, 1), 1: (1,), 3: (1,), 4: (2, 1), 6: (2, 1)}
GATHER_ORDER = (
    ("z", -1), ("z", 1), ("x", 0), ("first", 0), ("z", 3), ("z", -3), ("slots", 0), ("z", 2), ("z", -2),
    ("spread", 0), ("x", 1), ("first", -1), ("first", 1), ("x", -1), ("far", 0), ("z", -4), ("z", 4), ("x", 3),
    ("work", 0), ("x", -3), ("x", 2), ("x", -2), ("z", -6), ("z", 6), ("far", 1), ("far", -1), ("first", 2),
    ("first", -2), ("x", -4), ("x", 4), ("work", 1), ("far", 3), ("far", -3), ("work", -1), ("z", -5), ("far", 2),
    ("z", 5), ("first", 4), ("x", -6), ("first", -4), ("x", 6), ("z", -7), ("z", 7), ("far", -2), ("far", -4),
    ("work", 2), ("first", -3), ("first", 3), ("far", 4), ("work", -2), ("z", 8), ("work", -4), ("work", -3),
    ("x", -5), ("x", 5), ("far", -6), ("work", 3), ("first", 6), ("first", -6), ("far", 6), ("x", -7), ("work", 4),
    ("x", 7), ("x", 8), ("first", -5), ("first", 5), ("far", 5), ("far", -5), ("work", -6), ("work", 6), ("far", 7),
    ("far", -7), ("first", -7), ("work", 5), ("work", -5), ("first", 7), ("far", 8), ("first", 8), ("work", -7),
    ("work", 7), ("work", 8),
)
RING_ORDER = (
    ("ring", 0, 0), ("ring", 0, 1), ("ring", 0, 2), ("ring", -1, 0), ("ring", 1, 0), ("ring", -1, 1), ("ring", 1, 1),
    ("ring", 0, 3), ("ring", -1, 2), ("ring", 1, 2), ("ring", -3, 0), ("ring", 3, 0), ("ring", 3, 1), ("ring", -3, 1),
    ("ring", 2, 0), ("ring", -2, 0), ("ring", -2, 1), ("ring", -3, 2), ("ring", 2, 1), ("ring", -1, 3),
    ("ring", 3, 2), ("ring", 1, 3), ("ring", 4, 0), ("ring", -4, 0), ("ring", -3, 3), ("ring", 3, 3), ("ring", -4, 1),
    ("ring", 4, 1), ("ring", 2, 2), ("ring", -2, 2), ("ring", -2, 3), ("ring", 2, 3), ("ring", 4, 2), ("ring", -4, 2),
    ("ring", 5, 0), ("ring", 6, 0), ("ring", -5, 0), ("ring", 5, 1), ("ring", -4, 3), ("ring", 4, 3), ("ring", -5, 1),
    ("ring", -6, 0), ("ring", 6, 1), ("ring", 5, 2), ("ring", -6, 1), ("ring", -5, 2), ("ring", 6, 2),
    ("ring", -6, 2), ("ring", 7, 0), ("ring", -7, 0), ("ring", 8, 0), ("ring", 5, 3), ("ring", -5, 3),
    ("ring", -6, 3), ("ring", -7, 1), ("ring", 7, 1), ("ring", 6, 3), ("ring", -7, 2), ("sum", 0, 0), ("ring", 8, 1),
    ("ring", 7, 2), ("ring", 8, 2), ("sum", 0, 1), ("ring", -7, 3), ("ring", 7, 3), ("sum", 0, 2), ("ring", 8, 3),
    ("sum", 0, 3),
)


def sends_of(plan, offset):
    half = NZ // 2
    up = [k for k in plan.get(offset, ()) if offset >= 0 and offset + k <= half]
    down = [-k for k in plan.get(-offset, ()) if offset <= 0 and k - offset < half]
    return [k for pair in zip(up, down) for k in pair] if offset == 0 else up + down


def iota(shape, dim):
    return lax.broadcasted_iota(jnp.int32, shape, dim)


def dot_nt(a, b):
    return lax.dot_general(a, b, (((1,), (1,)), ((), ())), preferred_element_type=F32)


def dot(a, b):
    return jnp.dot(a, b, preferred_element_type=F32)


def kernel(
    amps_hbm,
    resid_hbm,
    block_hbm,
    energy_hbm,
    item_hbm,
    owner_hbm,
    pair_hbm,
    mate_hbm,
    pair_energy_hbm,
    twin_hbm,
    out_ref,
    turned,
    blocks,
    amp_all,
    slot_all,
    counts,
    spread,
    slotted,
    inter_acc,
    inter,
    w_send,
    w_recv,
    scaled,
    m_send,
    m_recv,
    ecol,
    amps_ref,
    resid,
    block_ref,
    energy_ref,
    item_ref,
    owner_ref,
    pair_ref,
    mate_ref,
    pair_energy_ref,
    twin_ref,
    local_sem,
    send_sem,
    y_recv,
    s_recv,
    n_recv,
    z_recv,
    f_recv,
    fx_recv,
    xw_recv,
    xh_recv,
    core_recv,
    g_recv,
    gc_recv,
    w_rsem,
    m_rsem,
):
    x = lax.axis_index("pairs_0")
    z = lax.axis_index("pairs_1")
    c = lax.axis_index("pairs_2")
    y = lax.axis_index("ints")
    mate = {"pairs_2": 1 - c}
    x_up = {"pairs_0": lax.rem(x + 1, NX)}
    x_down = {"pairs_0": lax.rem(x + NX - 1, NX)}

    def at_z(k):
        return {"pairs_1": lax.rem(z + k + NZ, NZ)}

    def at_xy(dx, dy):
        return {"pairs_0": lax.rem(x + dx, NX), "ints": lax.rem(y + dy, NY)}

    def remote(src, dst, ssem, rsem, device):
        return pltpu.make_async_remote_copy(
            src_ref=src, dst_ref=dst, send_sem=ssem, recv_sem=rsem, device_id=device, device_id_type=MESH
        )

    def await_bytes(ref, sem):
        pltpu.make_async_copy(ref, ref, sem).wait()

    held = (amps_hbm, resid_hbm, block_hbm, energy_hbm, item_hbm, owner_hbm, pair_hbm, mate_hbm, pair_energy_hbm, twin_hbm)
    used = (amps_ref, resid, block_ref, energy_ref, item_ref, owner_ref, pair_ref, mate_ref, pair_energy_ref, twin_ref)
    copies = [pltpu.make_async_copy(a, b, local_sem.at[i]) for i, (a, b) in enumerate(zip(held, used))]
    for i in (2, 0, 4, 5, 6, 7, 3, 8, 9, 1):
        copies[i].start()

    barrier = pltpu.get_barrier_semaphore()
    offsets = [(dx, dy) for dx in range(NX) for dy in range(NY) if dx or dy]
    z_steps = sorted({k for plan in (BLOCK_PLAN, FIRST_PLAN, RING_PLAN) for steps in plan.values() for k in steps})
    greeted = [at_z(k) for step in z_steps for k in (step, -step)] + [mate] + [at_xy(dx, dy) for dx, dy in offsets]
    for device in greeted:
        pl.semaphore_signal(barrier, inc=1, device_id=device, device_id_type=MESH)

    copies[2].wait()
    turned[...] = jnp.transpose(block_ref[...].astype(F32))
    blocks[x, z, c] = turned[pl.ds(pl.multiple_of(y * SL, SL), SL), :].astype(BF16)
    copies[0].wait()
    amp_all[y] = amps_ref[...].astype(BF16)

    copies[4].wait()
    n_items = item_ref.shape[1]
    twice = (iota((n_items, ROWS), 0) == iota((n_items, ROWS), 1) // 2).astype(F32).astype(BF16)
    item = jnp.broadcast_to(item_ref[...].astype(F32), (16, n_items)).astype(BF16)
    row = dot(item, twice)[0:1].astype(jnp.int32)
    square = jnp.broadcast_to(row, (ROWS, ROWS)).astype(F32)
    earlier = (jnp.transpose(square) == square) & (iota((ROWS, ROWS), 0) < iota((ROWS, ROWS), 1))
    rank = jnp.sum(earlier.astype(F32), axis=0, keepdims=True)
    z_of = (row >> 1) & (NZ - 1)
    place = z_of * (BLK8 * CAP) + ((row >> 5) * NC + (row & 1)) * CAP
    slot_all[y] = jnp.broadcast_to(place.astype(F32) + rank, (8, ROWS))

    for i in (5, 6, 7):
        copies[i].wait()
    n_req = owner_ref.shape[1]
    unit = owner_ref[...] * 2 + pair_ref[...]
    hot = (iota((V, n_req), 0) == unit).astype(F32).astype(BF16)
    out_id = iota((16, n_req), 0)
    mine = (iota((16, n_req), 1) // (n_req // 2)) * 2 + mate_ref[...]
    pick = (out_id == mine).astype(F32).astype(BF16)
    counts[x] = dot_nt(pick, hot).astype(BF16)

    pl.semaphore_wait(barrier, len(greeted))

    def send_piece(ref, ssem, rsem, device):
        remote(ref, ref, ssem, rsem, device).start()

    def z_of_piece(o):
        return lax.rem(z - o + NZ, NZ)

    rest, first_rows = pl.ds(FIRST, REST), pl.ds(0, FIRST)

    def z_piece(o):
        zz = z_of_piece(o)
        piece = blocks.at[x, zz, c, rest, :]
        if o:
            await_bytes(piece, z_recv.at[zz])
        for k in sends_of(BLOCK_PLAN, o):
            send_piece(piece, send_sem.at[0], z_recv.at[zz], at_z(k))
        send_piece(piece, send_sem.at[1], xw_recv.at[zz], x_up)
        send_piece(piece, send_sem.at[1], xw_recv.at[zz], x_down)
        send_piece(piece, send_sem.at[2], core_recv.at[zz], mate)

    def first_piece(o):
        zz = z_of_piece(o)
        piece = blocks.at[:, zz, c, first_rows, :]
        if o:
            await_bytes(piece, f_recv.at[zz])
        else:
            await_bytes(blocks.at[pl.ds(0, NX - 1), z, c, first_rows, :], fx_recv)
        for k in sends_of(FIRST_PLAN, o):
            send_piece(piece, send_sem.at[11], f_recv.at[zz], at_z(k))
        send_piece(piece, send_sem.at[2], core_recv.at[zz], mate)

    xl, xr, xo = lax.rem(x + NX - 1, NX), lax.rem(x + 1, NX), lax.rem(x + 2, NX)

    def halves(o):
        cut = FIRST + (2 * REST // 3 if o % 2 else REST // 3)
        return pl.ds(FIRST, cut - FIRST), pl.ds(cut, SL - cut)

    def x_piece(o):
        zz = z_of_piece(o)
        low, high = halves(o)
        await_bytes(blocks.at[pl.ds(0, 2), zz, c, rest, :], xw_recv.at[zz])
        send_piece(blocks.at[xl, zz, c, low, :], send_sem.at[1], xh_recv.at[zz], x_up)
        send_piece(blocks.at[xr, zz, c, high, :], send_sem.at[1], xh_recv.at[zz], x_down)
        send_piece(blocks.at[xl, zz, c, rest, :], send_sem.at[2], core_recv.at[zz], mate)
        send_piece(blocks.at[xr, zz, c, rest, :], send_sem.at[2], core_recv.at[zz], mate)

    def far_piece(o):
        zz = z_of_piece(o)
        piece = blocks.at[xo, zz, c, rest, :]
        await_bytes(piece, xh_recv.at[zz])
        send_piece(piece, send_sem.at[2], core_recv.at[zz], mate)

    group = BLK8 * CAP

    def slot_rows():
        await_bytes(slot_all.at[pl.ds(0, NY - 1)], s_recv)
        await_bytes(amp_all.at[pl.ds(0, NY - 1)], y_recv)
        for q in range(NY):
            slot_of = slot_all[q, 0:1, :]
            here = slot_of == iota((NZ * group, ROWS), 0).astype(F32)
            lane = iota((NZ * group, ROWS), 1)
            rows = amp_all[q]
            for p in range(2):
                own = here & ((lane >= SL) if p else (lane < SL))
                part = dot(own.astype(F32).astype(BF16), rows).astype(BF16)
                slotted[:, pl.ds(q * group, group), pl.ds(p * V, V)] = part.reshape(NZ, group, V)

    def spread_counts():
        await_bytes(counts.at[pl.ds(0, NX - 1)], n_recv)
        n_out = NX * 4
        tall = iota((n_out * EB, NX * 16), 0) // EB
        pick_row = (iota((n_out * EB, NX * 16), 1) == (tall // 4) * 16 + lax.rem(tall, 4)).astype(F32).astype(BF16)
        tall_counts = dot(pick_row, counts[...].reshape(NX * 16, V)).astype(BF16)
        wide = iota((V, UNITS * EB), 1) // EB + x * UNITS
        pick_col = (iota((V, UNITS * EB), 0) == wide).astype(F32).astype(BF16)
        full = dot(tall_counts, pick_col)
        same = lax.rem(iota(full.shape, 0), EB) == lax.rem(iota(full.shape, 1), EB)
        spread[...] = jnp.where(same, full, 0.0).astype(BF16)
        copies[3].wait()
        for p in range(2):
            ecol[p] = jnp.transpose(jnp.broadcast_to(energy_ref[p : p + 1, :], (128, V)))

    lane_block = lax.rem(iota((SL, SLOTS), 1), group) // CAP

    def block_work(o):
        zz = z_of_piece(o)
        await_bytes(blocks.at[:, zz, 1 - c], core_recv.at[zz])
        rows = slotted[zz]
        both_rows = rows[:, :V] + rows[:, V:]
        all_b = jnp.concatenate([blocks[k // NC, zz, k % NC] for k in range(BLK8)], axis=0)
        raw = dot_nt(all_b, both_rows)
        prod = jnp.zeros((SL, SLOTS), F32)
        for k in range(BLK8):
            prod = jnp.where(lane_block == k, raw[k * SL : (k + 1) * SL], prod)
        inter_acc[...] += dot(prod.astype(BF16), rows)

    for dx in range(1, NX):
        send_piece(blocks.at[x, z, c, first_rows, :], send_sem.at[12], fx_recv, at_xy(dx, 0))
    z_piece(0)
    for dy in range(1, NY):
        send_piece(slot_all.at[y], send_sem.at[3], s_recv, at_xy(0, dy))
        send_piece(amp_all.at[y], send_sem.at[4], y_recv, at_xy(0, dy))
    for dx in range(1, NX):
        send_piece(counts.at[x], send_sem.at[5], n_recv, at_xy(dx, 0))
    inter_acc[...] = jnp.zeros_like(inter_acc)

    for kind, o in GATHER_ORDER:
        if kind == "slots":
            slot_rows()
        elif kind == "spread":
            spread_counts()
        else:
            {"z": z_piece, "first": first_piece, "x": x_piece, "far": far_piece, "work": block_work}[kind](o)

    for eb in range(N_EB):
        for p in range(2):
            inter[eb, z, c, p] = inter_acc[pl.ds(eb * EB, EB), pl.ds(p * V, V)].astype(BF16)

    def ring_piece(o, eb):
        zz = z_of_piece(o)
        piece = inter.at[eb, zz, c]
        if o:
            await_bytes(piece, g_recv.at[eb, zz])
        for k in sends_of(RING_PLAN, o):
            send_piece(piece, send_sem.at[6], g_recv.at[eb, zz], at_z(k))
        send_piece(piece, send_sem.at[7], gc_recv.at[eb], mate)

    low_lane = iota((EB, 128), 1) < SL

    def sum_part(eb):
        await_bytes(inter.at[eb, :, 1 - c], gc_recv.at[eb])
        part = inter[eb].reshape(UNITS * EB, V)
        sums = dot(spread[...], part)
        for xd in range(NX):
            for p in range(2):
                base = (xd * 4 + p * 2) * EB
                first, second = sums[base : base + EB], sums[base + EB : base + 2 * EB]
                for yd in range(NY):
                    t = (yd // 2) * 128
                    f, g = first[:, t : t + 128], second[:, t : t + 128]
                    if yd % 2 == 0:
                        joined = jnp.where(low_lane, f, pltpu.roll(g, SL, 1))
                    else:
                        joined = jnp.where(low_lane, pltpu.roll(f, SL, 1), g)
                    w_send[xd, yd, eb, p] = joined.astype(BF16)
        for dx, dy in offsets:
            there = at_xy(dx, dy)
            remote(
                w_send.at[there["pairs_0"], there["ints"], eb],
                w_recv.at[dx, dy, eb],
                send_sem.at[8 if dx else 10],
                w_rsem.at[1 if dx else 0],
                there,
            ).start()

    for kind, o, eb in RING_ORDER:
        if kind == "ring":
            ring_piece(o, eb)
        else:
            sum_part(eb)

    w_recv[0, 0] = w_send[x, y]
    for i in (1, 8, 9):
        copies[i].wait()
    await_bytes(w_recv.at[0, pl.ds(1, NY - 1)], w_rsem.at[0])
    await_bytes(w_recv.at[pl.ds(1, NX - 1)], w_rsem.at[1])

    lane_low = iota((SL, 128), 1) < SL
    for p in range(2):
        parts = []
        for q in range(NY):
            dy = lax.rem(y - q + NY, NY)
            for eb in range(N_EB):
                parts.append(sum(w_recv[dx, dy, eb, p].astype(F32) for dx in range(NX)))
        w = jnp.transpose(jnp.concatenate(parts, axis=0)).astype(BF16)
        cycle = jnp.zeros((SL, V), F32)
        for j in range(2):
            rows = amp_all[:, pl.ds(j * SL, SL), :].reshape(V, V)
            cycle += dot(w[j * SL : (j + 1) * SL], rows)
        mine_rows = ecol[p, pl.ds(pl.multiple_of(y * SL, SL), SL), :]
        mine_rows = jnp.concatenate([mine_rows, mine_rows], axis=1)
        divisor = mine_rows + energy_ref[p : p + 1, :] - pair_energy_ref[p]
        scaled[p] = (resid[p] + cycle) / divisor
    for q in range(NY):
        t = (q // 2) * 128
        f, g = scaled[0, :, pl.ds(t, 128)], scaled[1, :, pl.ds(t, 128)]
        if q % 2 == 0:
            joined = jnp.where(lane_low, f, pltpu.roll(g, SL, 1))
        else:
            joined = jnp.where(lane_low, pltpu.roll(f, SL, 1), g)
        m_send[q] = joined.astype(BF16)
    for dy in range(NY):
        there = at_xy(NX // 2, dy)
        remote(m_send.at[there["ints"]], m_recv.at[dy], send_sem.at[9], m_rsem, there).start()
    await_bytes(m_recv, m_rsem)
    mirror = jnp.concatenate([m_recv[lax.rem(y - q + NY, NY)].astype(F32) for q in range(NY)], axis=0)
    mirror = jnp.transpose(mirror)
    first_twin = ((xo * NZ + z) * NC + c) * 2
    for p in range(2):
        which = jnp.full((SL, V), twin_ref[p] - first_twin)
        other = jnp.where(which == 1, mirror[SL:], mirror[:SL])
        out_ref[p] = -0.5 * (scaled[p] + other)

    await_bytes(blocks.at[0, pl.ds(0, NZ - 1), 0, rest, :], send_sem.at[0])
    await_bytes(blocks.at[pl.ds(0, NX - 1), :, 0, rest, :], send_sem.at[1])
    await_bytes(blocks.at[:, pl.ds(0, NZ - 1), 0, first_rows, :], send_sem.at[11])
    await_bytes(blocks.at[pl.ds(0, NX - 1), 0, 0, first_rows, :], send_sem.at[12])
    await_bytes(blocks.at[:, :, 0], send_sem.at[2])
    await_bytes(slot_all.at[pl.ds(0, NY - 1)], send_sem.at[3])
    await_bytes(amp_all.at[pl.ds(0, NY - 1)], send_sem.at[4])
    await_bytes(counts.at[pl.ds(0, NX - 1)], send_sem.at[5])
    await_bytes(inter.at[:, pl.ds(0, NZ - 1), 0], send_sem.at[6])
    await_bytes(inter.at[:, :, 0], send_sem.at[7])
    await_bytes(w_recv.at[pl.ds(0, NX - 1)], send_sem.at[8])
    await_bytes(w_recv.at[0, pl.ds(0, NY - 1)], send_sem.at[10])
    await_bytes(m_recv.at[:], send_sem.at[9])


def body(
    amps,
    resid_rest,
    int_blocks,
    virt_energy,
    pair_energy,
    item_block,
    share_owner,
    share_pair,
    share_amp,
    transpose_pair,
):
    n_items, n_req = item_block.shape[0], share_owner.shape[0]
    dma = pltpu.SemaphoreType.DMA
    return pl.pallas_call(
        kernel,
        out_shape=jax.ShapeDtypeStruct((2, SL, V), F32),
        in_specs=[pl.BlockSpec(memory_space=pltpu.HBM)] * 10,
        out_specs=pl.BlockSpec(memory_space=pltpu.VMEM),
        scratch_shapes=[
            pltpu.VMEM((V, V), F32),
            pltpu.VMEM((NX, NZ, NC, SL, V), BF16),
            pltpu.VMEM((NY, ROWS, V), BF16),
            pltpu.VMEM((NY, 8, ROWS), F32),
            pltpu.VMEM((NX, 16, V), BF16),
            pltpu.VMEM((NX * 4 * EB, UNITS * EB), BF16),
            pltpu.VMEM((NZ, SLOTS, 2 * V), BF16),
            pltpu.VMEM((SL, 2 * V), F32),
            pltpu.VMEM((N_EB, NZ, NC, 2, EB, V), BF16),
            pltpu.VMEM((NX, NY, N_EB, 2, EB, 128), BF16),
            pltpu.VMEM((NX, NY, N_EB, 2, EB, 128), BF16),
            pltpu.VMEM((2, SL, V), F32),
            pltpu.VMEM((NY, SL, 128), BF16),
            pltpu.VMEM((NY, SL, 128), BF16),
            pltpu.VMEM((2, V, 128), F32),
            pltpu.VMEM((ROWS, V), F32),
            pltpu.VMEM((2, SL, V), F32),
            pltpu.VMEM((V, V), BF16),
            pltpu.VMEM((2, V), F32),
            pltpu.VMEM((1, n_items), jnp.int32),
            pltpu.VMEM((1, n_req), jnp.int32),
            pltpu.VMEM((1, n_req), jnp.int32),
            pltpu.VMEM((1, n_req), jnp.int32),
            pltpu.SMEM((2,), F32),
            pltpu.SMEM((2,), jnp.int32),
            dma((10,)),
            dma((13,)),
            dma,
            dma,
            dma,
            dma((NZ,)),
            dma((NZ,)),
            dma,
            dma((NZ,)),
            dma((NZ,)),
            dma((NZ,)),
            dma((N_EB, NZ)),
            dma((N_EB,)),
            dma((2,)),
            dma,
        ],
        compiler_params=pltpu.CompilerParams(collective_id=0, has_side_effects=True, vmem_limit_bytes=24 * 2**20),
        name="cycle",
    )(
        *(
            pltpu.with_memory_space_constraint(operand, pltpu.HBM)
            for operand in (
                amps.reshape(ROWS, V),
                resid_rest,
                int_blocks[0],
                virt_energy,
                item_block.reshape(1, -1),
                share_owner.reshape(1, -1),
                share_pair.reshape(1, -1),
                share_amp.reshape(1, -1),
                pair_energy,
                transpose_pair,
            )
        )
    )


def solution(mesh):
    torus = Mesh(
        mesh.devices.reshape(NX, NZ, NC, mesh.shape["ints"]),
        ("pairs_0", "pairs_1", "pairs_2", "ints"),
    )
    return jax.shard_map(
        body,
        mesh=torus,
        in_specs=(
            P(PAIRS, "ints", None),
            P(PAIRS, "ints", None),
            P(PAIRS, None, None),
            P(PAIRS, None),
            P(PAIRS),
            P(PAIRS_INTS, None),
            P(PAIRS, None),
            P(PAIRS, None),
            P(PAIRS, None),
            P(PAIRS),
        ),
        out_specs=P(PAIRS, "ints", None),
        check_vma=False,
    )
```

```python
import functools

import jax
import jax.numpy as jnp
from jax import lax
from jax.experimental import pallas as pl
from jax.experimental.pallas import tpu as pltpu
from jax.sharding import Mesh
from jax.sharding import PartitionSpec as P

PAIRS = ("pairs_0", "pairs_1", "pairs_2")
PAIRS_INTS = ("pairs_0", "pairs_1", "pairs_2", "ints")
MESH = pl.DeviceIdType.MESH
F32 = jnp.float32
BF16 = jnp.bfloat16
NX, NZ, NC, NY = 4, 16, 2, 4
V = 256
SL = V // NY
ROWS = 2 * SL
HALF = SL // 2
CAP = 4
BLK8 = NX * NC
SLOTS = NY * BLK8 * CAP
UNITS = NZ * NC * 2
EB = 16
N_EB = SL // EB
FIRST = 16
REST = SL - FIRST
BLOCK_PLAN = {0: (1, 3), 1: (1,), 3: (1, 3), 4: (1,), 6: (1, 2)}
FIRST_PLAN = {0: (1,), 1: (3, 1), 2: (1,), 3: (2,), 4: (2,), 6: (2, 1)}
RING_PLAN = {0: (3, 1), 1: (1,), 3: (1,), 4: (2, 1), 6: (2, 1)}
GATHER_ORDER = (
    ("z", -1), ("z", 1), ("first", 0), ("x", 0), ("z", 3), ("z", -3), ("spread", 0), ("z", 2), ("z", -2), ("x", 1),
    ("first", 1), ("x", -1), ("first", -1), ("far", 0), ("slots", 0), ("z", 4), ("z", -4), ("x", 2), ("x", 3),
    ("x", -2), ("x", -3), ("work", 0), ("z", -6), ("z", 6), ("far", 1), ("far", -1), ("first", -2), ("x", -4),
    ("first", 2), ("x", 4), ("work", 1), ("z", 5), ("z", -5), ("far", 2), ("first", 4), ("far", -3), ("first", -4),
    ("x", -6), ("z", -7), ("work", -1), ("far", 3), ("z", 7), ("x", 6), ("far", -4), ("far", -2), ("work", 2),
    ("far", 4), ("first", -3), ("z", 8), ("first", 3), ("x", 5), ("x", -5), ("work", -3), ("far", -6), ("first", 6),
    ("work", -4), ("x", -7), ("work", -2), ("x", 7), ("first", -6), ("work", 3), ("x", 8), ("work", 4), ("first", -5),
    ("far", 6), ("first", 5), ("far", 5), ("far", -5), ("work", 6), ("work", -6), ("far", -7), ("far", 7),
    ("first", -7), ("first", 7), ("work", 5), ("far", 8), ("first", 8), ("work", -5), ("work", -7), ("work", 7),
    ("work", 8),
)
RING_ORDER = (
    ("ring", 0, 0), ("ring", 0, 1), ("ring", 0, 2), ("ring", -1, 1), ("ring", -1, 0), ("ring", 1, 0), ("ring", 1, 1),
    ("ring", 0, 3), ("ring", -1, 2), ("ring", -3, 0), ("ring", 3, 0), ("ring", 1, 2), ("ring", 3, 1), ("ring", -3, 1),
    ("ring", -3, 2), ("ring", -2, 0), ("ring", 2, 0), ("ring", 3, 2), ("ring", -2, 1), ("ring", -1, 3),
    ("ring", 1, 3), ("ring", 2, 1), ("ring", 4, 0), ("ring", -4, 0), ("ring", 3, 3), ("ring", -3, 3), ("ring", -2, 2),
    ("ring", 2, 2), ("ring", -4, 1), ("ring", 4, 1), ("ring", 2, 3), ("ring", 4, 2), ("ring", -4, 2), ("ring", 6, 0),
    ("ring", -4, 3), ("ring", -5, 0), ("ring", 4, 3), ("ring", -2, 3), ("ring", -6, 0), ("ring", 5, 0),
    ("ring", -5, 1), ("ring", 5, 1), ("ring", 6, 1), ("ring", 5, 2), ("ring", -6, 1), ("ring", 6, 2), ("ring", -6, 2),
    ("ring", 7, 0), ("ring", -5, 2), ("ring", -7, 0), ("ring", 8, 0), ("ring", -5, 3), ("ring", -6, 3),
    ("ring", 6, 3), ("ring", -7, 1), ("ring", 7, 1), ("sum", 0, 0), ("ring", 5, 3), ("ring", 8, 1), ("ring", 7, 2),
    ("ring", -7, 2), ("ring", 8, 2), ("sum", 0, 1), ("ring", -7, 3), ("sum", 0, 2), ("ring", 7, 3), ("ring", 8, 3),
    ("sum", 0, 3),
)


def sends_of(plan, offset):
    half = NZ // 2
    up = [k for k in plan.get(offset, ()) if offset >= 0 and offset + k <= half]
    down = [-k for k in plan.get(-offset, ()) if offset <= 0 and k - offset < half]
    return [k for pair in zip(up, down) for k in pair] if offset == 0 else up + down


def iota(shape, dim):
    return lax.broadcasted_iota(jnp.int32, shape, dim)


def dot_nt(a, b):
    return lax.dot_general(a, b, (((1,), (1,)), ((), ())), preferred_element_type=F32)


def dot(a, b):
    return jnp.dot(a, b, preferred_element_type=F32)


def kernel(
    amps_hbm,
    resid_hbm,
    block_hbm,
    energy_hbm,
    item_hbm,
    owner_hbm,
    pair_hbm,
    mate_hbm,
    pair_energy_hbm,
    twin_hbm,
    out_ref,
    turned,
    blocks,
    amp_all,
    slot_all,
    counts,
    spread,
    slotted,
    inter_acc,
    inter,
    w_send,
    w_recv,
    scaled,
    m_send,
    m_recv,
    ecol,
    amps_ref,
    resid,
    block_ref,
    energy_ref,
    item_ref,
    owner_ref,
    pair_ref,
    mate_ref,
    pair_energy_ref,
    twin_ref,
    local_sem,
    send_sem,
    y_recv,
    s_recv,
    n_recv,
    z_recv,
    f_recv,
    fx_recv,
    xw_recv,
    xh_recv,
    core_recv,
    g_recv,
    gc_recv,
    w_rsem,
    m_rsem,
):
    x = lax.axis_index("pairs_0")
    z = lax.axis_index("pairs_1")
    c = lax.axis_index("pairs_2")
    y = lax.axis_index("ints")
    mate = {"pairs_2": 1 - c}
    x_up = {"pairs_0": lax.rem(x + 1, NX)}
    x_down = {"pairs_0": lax.rem(x + NX - 1, NX)}

    def at_z(k):
        return {"pairs_1": lax.rem(z + k + NZ, NZ)}

    def at_xy(dx, dy):
        return {"pairs_0": lax.rem(x + dx, NX), "ints": lax.rem(y + dy, NY)}

    def remote(src, dst, ssem, rsem, device):
        return pltpu.make_async_remote_copy(
            src_ref=src, dst_ref=dst, send_sem=ssem, recv_sem=rsem, device_id=device, device_id_type=MESH
        )

    def await_bytes(ref, sem):
        pltpu.make_async_copy(ref, ref, sem).wait()

    barrier = pltpu.get_barrier_semaphore()
    offsets = [(dx, dy) for dx in range(NX) for dy in range(NY) if dx or dy]
    z_steps = sorted({k for plan in (BLOCK_PLAN, FIRST_PLAN, RING_PLAN) for steps in plan.values() for k in steps})
    greeted = [at_xy(dx, dy) for dx, dy in sorted(offsets, key=lambda d: d[0] % 2 + d[1] % 2)]
    greeted += [at_z(k) for step in z_steps[::-1] for k in (step, -step)] + [mate]
    for device in greeted:
        pl.semaphore_signal(barrier, inc=1, device_id=device, device_id_type=MESH)

    held = (amps_hbm, resid_hbm, block_hbm, energy_hbm, item_hbm, owner_hbm, pair_hbm, mate_hbm, pair_energy_hbm, twin_hbm)
    used = (amps_ref, resid, block_ref, energy_ref, item_ref, owner_ref, pair_ref, mate_ref, pair_energy_ref, twin_ref)
    copies = [pltpu.make_async_copy(a, b, local_sem.at[i]) for i, (a, b) in enumerate(zip(held, used))]
    for i in (2, 0, 4, 5, 6, 7, 3, 8, 9, 1):
        copies[i].start()

    copies[2].wait()
    turned[...] = jnp.transpose(block_ref[...].astype(F32))
    blocks[x, z, c] = turned[pl.ds(pl.multiple_of(y * SL, SL), SL), :].astype(BF16)
    copies[0].wait()
    amp_all[y] = amps_ref[...].astype(BF16)

    copies[4].wait()
    n_items = item_ref.shape[1]
    twice = (iota((n_items, ROWS), 0) == iota((n_items, ROWS), 1) // 2).astype(F32).astype(BF16)
    item = jnp.broadcast_to(item_ref[...].astype(F32), (16, n_items)).astype(BF16)
    row = dot(item, twice)[0:1].astype(jnp.int32)
    square = jnp.broadcast_to(row, (ROWS, ROWS)).astype(F32)
    earlier = (jnp.transpose(square) == square) & (iota((ROWS, ROWS), 0) < iota((ROWS, ROWS), 1))
    rank = jnp.sum(earlier.astype(F32), axis=0, keepdims=True)
    z_of = (row >> 1) & (NZ - 1)
    place = z_of * (BLK8 * CAP) + ((row >> 5) * NC + (row & 1)) * CAP
    slot_all[y] = jnp.broadcast_to(place.astype(F32) + rank, (8, ROWS))

    for i in (5, 6, 7):
        copies[i].wait()
    n_req = owner_ref.shape[1]
    unit = owner_ref[...] * 2 + pair_ref[...]
    hot = (iota((V, n_req), 0) == unit).astype(F32).astype(BF16)
    out_id = iota((16, n_req), 0)
    mine = (iota((16, n_req), 1) // (n_req // 2)) * 2 + mate_ref[...]
    pick = (out_id == mine).astype(F32).astype(BF16)
    counts[x] = dot_nt(pick, hot).astype(BF16)

    pl.semaphore_wait(barrier, len(greeted))

    def send_piece(ref, ssem, rsem, device):
        remote(ref, ref, ssem, rsem, device).start()

    def z_of_piece(o):
        return lax.rem(z - o + NZ, NZ)

    rest, first_rows = pl.ds(FIRST, REST), pl.ds(0, FIRST)

    def z_piece(o):
        zz = z_of_piece(o)
        piece = blocks.at[x, zz, c, rest, :]
        if o:
            await_bytes(piece, z_recv.at[zz])
        for k in sends_of(BLOCK_PLAN, o):
            send_piece(piece, send_sem.at[0], z_recv.at[zz], at_z(k))
        send_piece(piece, send_sem.at[1], xw_recv.at[zz], x_up)
        send_piece(piece, send_sem.at[1], xw_recv.at[zz], x_down)
        send_piece(piece, send_sem.at[2], core_recv.at[zz], mate)

    def first_piece(o):
        zz = z_of_piece(o)
        piece = blocks.at[:, zz, c, first_rows, :]
        if o:
            await_bytes(piece, f_recv.at[zz])
        else:
            await_bytes(blocks.at[pl.ds(0, NX - 1), z, c, first_rows, :], fx_recv)
        for k in sends_of(FIRST_PLAN, o):
            send_piece(piece, send_sem.at[11], f_recv.at[zz], at_z(k))
        send_piece(piece, send_sem.at[2], core_recv.at[zz], mate)

    xl, xr, xo = lax.rem(x + NX - 1, NX), lax.rem(x + 1, NX), lax.rem(x + 2, NX)

    def halves(o):
        cut = FIRST + (2 * REST // 3 if o % 2 else REST // 3)
        return pl.ds(FIRST, cut - FIRST), pl.ds(cut, SL - cut)

    def x_piece(o):
        zz = z_of_piece(o)
        low, high = halves(o)
        await_bytes(blocks.at[pl.ds(0, 2), zz, c, rest, :], xw_recv.at[zz])
        send_piece(blocks.at[xl, zz, c, low, :], send_sem.at[1], xh_recv.at[zz], x_up)
        send_piece(blocks.at[xr, zz, c, high, :], send_sem.at[1], xh_recv.at[zz], x_down)
        send_piece(blocks.at[xl, zz, c, rest, :], send_sem.at[2], core_recv.at[zz], mate)
        send_piece(blocks.at[xr, zz, c, rest, :], send_sem.at[2], core_recv.at[zz], mate)

    def far_piece(o):
        zz = z_of_piece(o)
        piece = blocks.at[xo, zz, c, rest, :]
        await_bytes(piece, xh_recv.at[zz])
        send_piece(piece, send_sem.at[2], core_recv.at[zz], mate)

    group = BLK8 * CAP

    def slot_rows():
        await_bytes(slot_all.at[pl.ds(0, NY - 1)], s_recv)
        await_bytes(amp_all.at[pl.ds(0, NY - 1)], y_recv)
        for q in range(NY):
            slot_of = slot_all[q, 0:1, :]
            here = slot_of == iota((NZ * group, ROWS), 0).astype(F32)
            lane = iota((NZ * group, ROWS), 1)
            rows = amp_all[q]
            for p in range(2):
                own = here & ((lane >= SL) if p else (lane < SL))
                part = dot(own.astype(F32).astype(BF16), rows).astype(BF16)
                slotted[:, pl.ds(q * group, group), pl.ds(p * V, V)] = part.reshape(NZ, group, V)

    def spread_counts():
        await_bytes(counts.at[pl.ds(0, NX - 1)], n_recv)
        n_out = NX * 4
        tall = iota((n_out * EB, NX * 16), 0) // EB
        pick_row = (iota((n_out * EB, NX * 16), 1) == (tall // 4) * 16 + lax.rem(tall, 4)).astype(F32).astype(BF16)
        tall_counts = dot(pick_row, counts[...].reshape(NX * 16, V)).astype(BF16)
        wide = iota((V, UNITS * EB), 1) // EB + x * UNITS
        pick_col = (iota((V, UNITS * EB), 0) == wide).astype(F32).astype(BF16)
        full = dot(tall_counts, pick_col)
        same = lax.rem(iota(full.shape, 0), EB) == lax.rem(iota(full.shape, 1), EB)
        spread[...] = jnp.where(same, full, 0.0).astype(BF16)
        copies[3].wait()
        for p in range(2):
            ecol[p] = jnp.transpose(jnp.broadcast_to(energy_ref[p : p + 1, :], (128, V)))

    lane_block = lax.rem(iota((SL, SLOTS), 1), group) // CAP

    def block_work(o):
        zz = z_of_piece(o)
        await_bytes(blocks.at[:, zz, 1 - c], core_recv.at[zz])
        rows = slotted[zz]
        both_rows = rows[:, :V] + rows[:, V:]
        all_b = jnp.concatenate([blocks[k // NC, zz, k % NC] for k in range(BLK8)], axis=0)
        raw = dot_nt(all_b, both_rows)
        prod = jnp.zeros((SL, SLOTS), F32)
        for k in range(BLK8):
            prod = jnp.where(lane_block == k, raw[k * SL : (k + 1) * SL], prod)
        inter_acc[...] += dot(prod.astype(BF16), rows)

    for dx in range(1, NX):
        send_piece(blocks.at[x, z, c, first_rows, :], send_sem.at[12], fx_recv, at_xy(dx, 0))
    z_piece(0)
    for dy in range(1, NY):
        send_piece(slot_all.at[y], send_sem.at[3], s_recv, at_xy(0, dy))
        send_piece(amp_all.at[y], send_sem.at[4], y_recv, at_xy(0, dy))
    for dx in range(1, NX):
        send_piece(counts.at[x], send_sem.at[5], n_recv, at_xy(dx, 0))
    inter_acc[...] = jnp.zeros_like(inter_acc)

    for kind, o in GATHER_ORDER:
        if kind == "slots":
            slot_rows()
        elif kind == "spread":
            spread_counts()
        else:
            {"z": z_piece, "first": first_piece, "x": x_piece, "far": far_piece, "work": block_work}[kind](o)

    for eb in range(N_EB):
        for p in range(2):
            inter[eb, z, c, p] = inter_acc[pl.ds(eb * EB, EB), pl.ds(p * V, V)].astype(BF16)

    def ring_piece(o, eb):
        zz = z_of_piece(o)
        piece = inter.at[eb, zz, c]
        if o:
            await_bytes(piece, g_recv.at[eb, zz])
        for k in sends_of(RING_PLAN, o):
            send_piece(piece, send_sem.at[6], g_recv.at[eb, zz], at_z(k))
        send_piece(piece, send_sem.at[7], gc_recv.at[eb], mate)

    low_lane = iota((EB, 128), 1) < SL

    def sum_part(eb):
        await_bytes(inter.at[eb, :, 1 - c], gc_recv.at[eb])
        part = inter[eb].reshape(UNITS * EB, V)
        sums = dot(spread[...], part)
        for xd in range(NX):
            for p in range(2):
                base = (xd * 4 + p * 2) * EB
                first, second = sums[base : base + EB], sums[base + EB : base + 2 * EB]
                for yd in range(NY):
                    t = (yd // 2) * 128
                    f, g = first[:, t : t + 128], second[:, t : t + 128]
                    if yd % 2 == 0:
                        joined = jnp.where(low_lane, f, pltpu.roll(g, SL, 1))
                    else:
                        joined = jnp.where(low_lane, pltpu.roll(f, SL, 1), g)
                    w_send[xd, yd, eb, p] = joined.astype(BF16)
        for dx, dy in offsets:
            there = at_xy(dx, dy)
            remote(
                w_send.at[there["pairs_0"], there["ints"], eb],
                w_recv.at[dx, dy, eb],
                send_sem.at[8 if dx else 10],
                w_rsem.at[1 if dx else 0],
                there,
            ).start()

    for kind, o, eb in RING_ORDER:
        if kind == "ring":
            ring_piece(o, eb)
        else:
            sum_part(eb)

    w_recv[0, 0] = w_send[x, y]
    for i in (1, 8, 9):
        copies[i].wait()
    await_bytes(w_recv.at[0, pl.ds(1, NY - 1)], w_rsem.at[0])
    await_bytes(w_recv.at[pl.ds(1, NX - 1)], w_rsem.at[1])

    lane_low = iota((SL, 128), 1) < SL
    for p in range(2):
        parts = []
        for q in range(NY):
            dy = lax.rem(y - q + NY, NY)
            for eb in range(N_EB):
                parts.append(sum(w_recv[dx, dy, eb, p].astype(F32) for dx in range(NX)))
        w = jnp.transpose(jnp.concatenate(parts, axis=0)).astype(BF16)
        cycle = jnp.zeros((SL, V), F32)
        for j in range(2):
            rows = amp_all[:, pl.ds(j * SL, SL), :].reshape(V, V)
            cycle += dot(w[j * SL : (j + 1) * SL], rows)
        mine_rows = ecol[p, pl.ds(pl.multiple_of(y * SL, SL), SL), :]
        mine_rows = jnp.concatenate([mine_rows, mine_rows], axis=1)
        divisor = mine_rows + energy_ref[p : p + 1, :] - pair_energy_ref[p]
        scaled[p] = (resid[p] + cycle) / divisor
    for q in range(NY):
        t = (q // 2) * 128
        f, g = scaled[0, :, pl.ds(t, 128)], scaled[1, :, pl.ds(t, 128)]
        if q % 2 == 0:
            joined = jnp.where(lane_low, f, pltpu.roll(g, SL, 1))
        else:
            joined = jnp.where(lane_low, pltpu.roll(f, SL, 1), g)
        m_send[q] = joined.astype(BF16)
    for dy in range(NY):
        there = at_xy(NX // 2, dy)
        remote(m_send.at[there["ints"]], m_recv.at[dy], send_sem.at[9], m_rsem, there).start()
    await_bytes(m_recv, m_rsem)
    mirror = jnp.concatenate([m_recv[lax.rem(y - q + NY, NY)].astype(F32) for q in range(NY)], axis=0)
    mirror = jnp.transpose(mirror)
    first_twin = ((xo * NZ + z) * NC + c) * 2
    for p in range(2):
        which = jnp.full((SL, V), twin_ref[p] - first_twin)
        other = jnp.where(which == 1, mirror[SL:], mirror[:SL])
        out_ref[p] = -0.5 * (scaled[p] + other)

    await_bytes(blocks.at[0, pl.ds(0, NZ - 1), 0, rest, :], send_sem.at[0])
    await_bytes(blocks.at[pl.ds(0, NX - 1), :, 0, rest, :], send_sem.at[1])
    await_bytes(blocks.at[:, pl.ds(0, NZ - 1), 0, first_rows, :], send_sem.at[11])
    await_bytes(blocks.at[pl.ds(0, NX - 1), 0, 0, first_rows, :], send_sem.at[12])
    await_bytes(blocks.at[:, :, 0], send_sem.at[2])
    await_bytes(slot_all.at[pl.ds(0, NY - 1)], send_sem.at[3])
    await_bytes(amp_all.at[pl.ds(0, NY - 1)], send_sem.at[4])
    await_bytes(counts.at[pl.ds(0, NX - 1)], send_sem.at[5])
    await_bytes(inter.at[:, pl.ds(0, NZ - 1), 0], send_sem.at[6])
    await_bytes(inter.at[:, :, 0], send_sem.at[7])
    await_bytes(w_recv.at[pl.ds(0, NX - 1)], send_sem.at[8])
    await_bytes(w_recv.at[0, pl.ds(0, NY - 1)], send_sem.at[10])
    await_bytes(m_recv.at[:], send_sem.at[9])


def body(
    amps,
    resid_rest,
    int_blocks,
    virt_energy,
    pair_energy,
    item_block,
    share_owner,
    share_pair,
    share_amp,
    transpose_pair,
):
    n_items, n_req = item_block.shape[0], share_owner.shape[0]
    dma = pltpu.SemaphoreType.DMA
    return pl.pallas_call(
        kernel,
        out_shape=jax.ShapeDtypeStruct((2, SL, V), F32),
        in_specs=[pl.BlockSpec(memory_space=pltpu.HBM)] * 10,
        out_specs=pl.BlockSpec(memory_space=pltpu.VMEM),
        scratch_shapes=[
            pltpu.VMEM((V, V), F32),
            pltpu.VMEM((NX, NZ, NC, SL, V), BF16),
            pltpu.VMEM((NY, ROWS, V), BF16),
            pltpu.VMEM((NY, 8, ROWS), F32),
            pltpu.VMEM((NX, 16, V), BF16),
            pltpu.VMEM((NX * 4 * EB, UNITS * EB), BF16),
            pltpu.VMEM((NZ, SLOTS, 2 * V), BF16),
            pltpu.VMEM((SL, 2 * V), F32),
            pltpu.VMEM((N_EB, NZ, NC, 2, EB, V), BF16),
            pltpu.VMEM((NX, NY, N_EB, 2, EB, 128), BF16),
            pltpu.VMEM((NX, NY, N_EB, 2, EB, 128), BF16),
            pltpu.VMEM((2, SL, V), F32),
            pltpu.VMEM((NY, SL, 128), BF16),
            pltpu.VMEM((NY, SL, 128), BF16),
            pltpu.VMEM((2, V, 128), F32),
            pltpu.VMEM((ROWS, V), F32),
            pltpu.VMEM((2, SL, V), F32),
            pltpu.VMEM((V, V), BF16),
            pltpu.VMEM((2, V), F32),
            pltpu.VMEM((1, n_items), jnp.int32),
            pltpu.VMEM((1, n_req), jnp.int32),
            pltpu.VMEM((1, n_req), jnp.int32),
            pltpu.VMEM((1, n_req), jnp.int32),
            pltpu.SMEM((2,), F32),
            pltpu.SMEM((2,), jnp.int32),
            dma((10,)),
            dma((13,)),
            dma,
            dma,
            dma,
            dma((NZ,)),
            dma((NZ,)),
            dma,
            dma((NZ,)),
            dma((NZ,)),
            dma((NZ,)),
            dma((N_EB, NZ)),
            dma((N_EB,)),
            dma((2,)),
            dma,
        ],
        compiler_params=pltpu.CompilerParams(collective_id=0, has_side_effects=True, vmem_limit_bytes=24 * 2**20),
        name="cycle",
    )(
        *(
            pltpu.with_memory_space_constraint(operand, pltpu.HBM)
            for operand in (
                amps.reshape(ROWS, V),
                resid_rest,
                int_blocks[0],
                virt_energy,
                item_block.reshape(1, -1),
                share_owner.reshape(1, -1),
                share_pair.reshape(1, -1),
                share_amp.reshape(1, -1),
                pair_energy,
                transpose_pair,
            )
        )
    )


def solution(mesh):
    torus = Mesh(
        mesh.devices.reshape(NX, NZ, NC, mesh.shape["ints"]),
        ("pairs_0", "pairs_1", "pairs_2", "ints"),
    )
    return jax.shard_map(
        body,
        mesh=torus,
        in_specs=(
            P(PAIRS, "ints", None),
            P(PAIRS, "ints", None),
            P(PAIRS, None, None),
            P(PAIRS, None),
            P(PAIRS),
            P(PAIRS_INTS, None),
            P(PAIRS, None),
            P(PAIRS, None),
            P(PAIRS, None),
            P(PAIRS),
        ),
        out_specs=P(PAIRS, "ints", None),
        check_vma=False,
    )
```

```python
import functools

import jax
import jax.numpy as jnp
from jax import lax
from jax.experimental import pallas as pl
from jax.experimental.pallas import tpu as pltpu
from jax.sharding import Mesh
from jax.sharding import PartitionSpec as P

PAIRS = ("pairs_0", "pairs_1", "pairs_2")
PAIRS_INTS = ("pairs_0", "pairs_1", "pairs_2", "ints")
MESH = pl.DeviceIdType.MESH
F32 = jnp.float32
BF16 = jnp.bfloat16
NX, NZ, NC, NY = 4, 16, 2, 4
V = 256
SL = V // NY
ROWS = 2 * SL
HALF = SL // 2
CAP = 4
BLK8 = NX * NC
SLOTS = NY * BLK8 * CAP
UNITS = NZ * NC * 2
EB = 16
N_EB = SL // EB
FIRST = 16
REST = SL - FIRST
BLOCK_PLAN = {0: (1, 3), 1: (1,), 3: (1, 3), 4: (1,), 6: (1, 2)}
FIRST_PLAN = {0: (1,), 1: (3, 1), 2: (1,), 3: (2,), 4: (2,), 6: (2, 1)}
RING_PLAN = {0: (3, 1), 1: (1,), 3: (1,), 4: (2, 1), 6: (2, 1)}
GATHER_ORDER = (
    ("x", 0), ("z", -1), ("z", 1), ("first", 0), ("z", 3), ("z", -3), ("spread", 0), ("z", 2), ("z", -2),
    ("first", 1), ("x", 1), ("x", -1), ("first", -1), ("z", -4), ("z", 4), ("x", -3), ("x", 3), ("x", 2), ("z", -6),
    ("x", -2), ("far", 0), ("slots", 0), ("z", 6), ("far", 1), ("far", -1), ("x", -4), ("first", 2), ("first", -2),
    ("x", 4), ("z", 5), ("work", -1), ("z", -5), ("far", -3), ("far", 2), ("first", 4), ("x", -6), ("work", 0),
    ("z", -7), ("x", 6), ("first", -4), ("far", -4), ("z", 7), ("far", 3), ("far", -2), ("work", 1), ("work", 2),
    ("far", 4), ("first", 3), ("z", 8), ("first", -3), ("x", 5), ("work", -4), ("work", -2), ("x", -5), ("far", -6),
    ("first", 6), ("x", -7), ("work", 3), ("x", 7), ("first", -6), ("work", 4), ("far", 6), ("x", 8), ("work", -3),
    ("first", 5), ("far", 5), ("first", -5), ("far", -5), ("work", -6), ("work", 6), ("work", 5), ("far", 7),
    ("far", -7), ("first", 7), ("first", -7), ("first", 8), ("far", 8), ("work", -5), ("work", 7), ("work", -7),
    ("work", 8),
)
RING_ORDER = (
    ("ring", 0, 0), ("ring", 0, 1), ("ring", 0, 2), ("ring", -1, 0), ("ring", 1, 0), ("ring", -1, 1), ("ring", 1, 1),
    ("ring", 0, 3), ("ring", 3, 0), ("ring", -3, 0), ("ring", 1, 2), ("ring", 3, 1), ("ring", -3, 1), ("ring", 2, 0),
    ("ring", -1, 2), ("ring", -2, 0), ("ring", -2, 1), ("ring", -3, 2), ("ring", -1, 3), ("ring", 3, 2),
    ("ring", 1, 3), ("ring", 4, 0), ("ring", -4, 0), ("ring", -3, 3), ("ring", 3, 3), ("ring", 2, 1), ("ring", 2, 2),
    ("ring", -4, 1), ("ring", 4, 1), ("ring", -2, 2), ("ring", 4, 2), ("ring", 2, 3), ("ring", -4, 2), ("ring", 6, 0),
    ("ring", -5, 0), ("ring", -6, 0), ("ring", -4, 3), ("ring", 5, 1), ("ring", 4, 3), ("ring", -2, 3),
    ("ring", 6, 1), ("ring", -6, 1), ("ring", 5, 0), ("ring", -6, 2), ("ring", 5, 2), ("ring", -5, 1), ("ring", 6, 2),
    ("ring", 7, 0), ("ring", -7, 0), ("ring", 8, 0), ("ring", 5, 3), ("ring", -6, 3), ("ring", 6, 3), ("ring", -5, 2),
    ("ring", -7, 1), ("ring", -5, 3), ("ring", 7, 1), ("ring", -7, 2), ("ring", 8, 1), ("sum", 0, 0), ("ring", 8, 2),
    ("ring", 7, 2), ("sum", 0, 1), ("ring", -7, 3), ("sum", 0, 2), ("ring", 7, 3), ("ring", 8, 3), ("sum", 0, 3),
)


def sends_of(plan, offset):
    half = NZ // 2
    up = [k for k in plan.get(offset, ()) if offset >= 0 and offset + k <= half]
    down = [-k for k in plan.get(-offset, ()) if offset <= 0 and k - offset < half]
    return [k for pair in zip(up, down) for k in pair] if offset == 0 else up + down


def iota(shape, dim):
    return lax.broadcasted_iota(jnp.int32, shape, dim)


def dot_nt(a, b):
    return lax.dot_general(a, b, (((1,), (1,)), ((), ())), preferred_element_type=F32)


def dot(a, b):
    return jnp.dot(a, b, preferred_element_type=F32)


def kernel(
    amps_hbm,
    resid_hbm,
    block_hbm,
    energy_hbm,
    item_hbm,
    owner_hbm,
    pair_hbm,
    mate_hbm,
    pair_energy_hbm,
    twin_hbm,
    out_ref,
    turned,
    blocks,
    amp_all,
    slot_all,
    counts,
    spread,
    slotted,
    inter_acc,
    inter,
    w_send,
    w_recv,
    scaled,
    m_send,
    m_recv,
    ecol,
    amps_ref,
    resid,
    block_ref,
    energy_ref,
    item_ref,
    owner_ref,
    pair_ref,
    mate_ref,
    pair_energy_ref,
    twin_ref,
    local_sem,
    send_sem,
    y_recv,
    s_recv,
    n_recv,
    z_recv,
    f_recv,
    fx_recv,
    xw_recv,
    xh_recv,
    core_recv,
    g_recv,
    gc_recv,
    w_rsem,
    m_rsem,
):
    x = lax.axis_index("pairs_0")
    z = lax.axis_index("pairs_1")
    c = lax.axis_index("pairs_2")
    y = lax.axis_index("ints")
    mate = {"pairs_2": 1 - c}
    x_up = {"pairs_0": lax.rem(x + 1, NX)}
    x_down = {"pairs_0": lax.rem(x + NX - 1, NX)}

    def at_z(k):
        return {"pairs_1": lax.rem(z + k + NZ, NZ)}

    def at_xy(dx, dy):
        return {"pairs_0": lax.rem(x + dx, NX), "ints": lax.rem(y + dy, NY)}

    def remote(src, dst, ssem, rsem, device):
        return pltpu.make_async_remote_copy(
            src_ref=src, dst_ref=dst, send_sem=ssem, recv_sem=rsem, device_id=device, device_id_type=MESH
        )

    def await_bytes(ref, sem):
        pltpu.make_async_copy(ref, ref, sem).wait()

    barrier = pltpu.get_barrier_semaphore()
    offsets = [(dx, dy) for dx in range(NX) for dy in range(NY) if dx or dy]
    z_steps = sorted({k for plan in (BLOCK_PLAN, FIRST_PLAN, RING_PLAN) for steps in plan.values() for k in steps})
    greeted = [at_xy(dx, dy) for dx, dy in sorted(offsets, key=lambda d: d[0] % 2 + d[1] % 2)]
    greeted += [at_z(k) for step in z_steps[::-1] for k in (step, -step)] + [mate]
    for device in greeted:
        pl.semaphore_signal(barrier, inc=1, device_id=device, device_id_type=MESH)

    held = (amps_hbm, resid_hbm, block_hbm, energy_hbm, item_hbm, owner_hbm, pair_hbm, mate_hbm, pair_energy_hbm, twin_hbm)
    used = (amps_ref, resid, block_ref, energy_ref, item_ref, owner_ref, pair_ref, mate_ref, pair_energy_ref, twin_ref)
    copies = [pltpu.make_async_copy(a, b, local_sem.at[i]) for i, (a, b) in enumerate(zip(held, used))]
    for i in (2, 0, 4, 5, 6, 7, 3, 8, 9, 1):
        copies[i].start()

    copies[2].wait()
    turned[...] = jnp.transpose(block_ref[...].astype(F32))
    blocks[x, z, c] = turned[pl.ds(pl.multiple_of(y * SL, SL), SL), :].astype(BF16)
    pl.semaphore_wait(barrier, len(greeted))

    def send_piece(ref, ssem, rsem, device):
        remote(ref, ref, ssem, rsem, device).start()

    def z_of_piece(o):
        return lax.rem(z - o + NZ, NZ)

    rest, first_rows = pl.ds(FIRST, REST), pl.ds(0, FIRST)

    def z_piece(o):
        zz = z_of_piece(o)
        piece = blocks.at[x, zz, c, rest, :]
        if o:
            await_bytes(piece, z_recv.at[zz])
        for k in sends_of(BLOCK_PLAN, o):
            send_piece(piece, send_sem.at[0], z_recv.at[zz], at_z(k))
        send_piece(piece, send_sem.at[1], xw_recv.at[zz], x_up)
        send_piece(piece, send_sem.at[1], xw_recv.at[zz], x_down)
        send_piece(piece, send_sem.at[2], core_recv.at[zz], mate)

    def first_piece(o):
        zz = z_of_piece(o)
        piece = blocks.at[:, zz, c, first_rows, :]
        if o:
            await_bytes(piece, f_recv.at[zz])
        else:
            await_bytes(blocks.at[pl.ds(0, NX - 1), z, c, first_rows, :], fx_recv)
        for k in sends_of(FIRST_PLAN, o):
            send_piece(piece, send_sem.at[11], f_recv.at[zz], at_z(k))
        send_piece(piece, send_sem.at[2], core_recv.at[zz], mate)

    xl, xr, xo = lax.rem(x + NX - 1, NX), lax.rem(x + 1, NX), lax.rem(x + 2, NX)

    def halves(o):
        cut = FIRST + (2 * REST // 3 if o % 2 else REST // 3)
        return pl.ds(FIRST, cut - FIRST), pl.ds(cut, SL - cut)

    def x_piece(o):
        zz = z_of_piece(o)
        low, high = halves(o)
        await_bytes(blocks.at[pl.ds(0, 2), zz, c, rest, :], xw_recv.at[zz])
        send_piece(blocks.at[xl, zz, c, low, :], send_sem.at[1], xh_recv.at[zz], x_up)
        send_piece(blocks.at[xr, zz, c, high, :], send_sem.at[1], xh_recv.at[zz], x_down)
        send_piece(blocks.at[xl, zz, c, rest, :], send_sem.at[2], core_recv.at[zz], mate)
        send_piece(blocks.at[xr, zz, c, rest, :], send_sem.at[2], core_recv.at[zz], mate)

    def far_piece(o):
        zz = z_of_piece(o)
        piece = blocks.at[xo, zz, c, rest, :]
        await_bytes(piece, xh_recv.at[zz])
        send_piece(piece, send_sem.at[2], core_recv.at[zz], mate)

    group = BLK8 * CAP

    def slot_rows():
        await_bytes(slot_all.at[pl.ds(0, NY - 1)], s_recv)
        await_bytes(amp_all.at[pl.ds(0, NY - 1)], y_recv)
        for q in range(NY):
            slot_of = slot_all[q, 0:1, :]
            here = slot_of == iota((NZ * group, ROWS), 0).astype(F32)
            lane = iota((NZ * group, ROWS), 1)
            rows = amp_all[q]
            for p in range(2):
                own = here & ((lane >= SL) if p else (lane < SL))
                part = dot(own.astype(F32).astype(BF16), rows).astype(BF16)
                slotted[:, pl.ds(q * group, group), pl.ds(p * V, V)] = part.reshape(NZ, group, V)

    def spread_counts():
        await_bytes(counts.at[pl.ds(0, NX - 1)], n_recv)
        n_out = NX * 4
        tall = iota((n_out * EB, NX * 16), 0) // EB
        pick_row = (iota((n_out * EB, NX * 16), 1) == (tall // 4) * 16 + lax.rem(tall, 4)).astype(F32).astype(BF16)
        tall_counts = dot(pick_row, counts[...].reshape(NX * 16, V)).astype(BF16)
        half = UNITS // NC * EB
        place = iota((V, half), 1) // EB
        for core in range(NC):
            wide = (place // 2) * (NC * 2) + core * 2 + lax.rem(place, 2) + x * UNITS
            pick_col = (iota((V, half), 0) == wide).astype(F32).astype(BF16)
            full = dot(tall_counts, pick_col)
            same = lax.rem(iota(full.shape, 0), EB) == lax.rem(iota(full.shape, 1), EB)
            spread[core] = jnp.where(same, full, 0.0).astype(BF16)
        copies[3].wait()
        for p in range(2):
            ecol[p] = jnp.transpose(jnp.broadcast_to(energy_ref[p : p + 1, :], (128, V)))

    lane_block = lax.rem(iota((SL, SLOTS), 1), group) // CAP

    def block_work(o):
        zz = z_of_piece(o)
        await_bytes(blocks.at[:, zz, 1 - c], core_recv.at[zz])
        rows = slotted[zz]
        both_rows = rows[:, :V] + rows[:, V:]
        all_b = jnp.concatenate([blocks[k // NC, zz, k % NC] for k in range(BLK8)], axis=0)
        raw = dot_nt(all_b, both_rows)
        prod = jnp.zeros((SL, SLOTS), F32)
        for k in range(BLK8):
            prod = jnp.where(lane_block == k, raw[k * SL : (k + 1) * SL], prod)
        inter_acc[...] += dot(prod.astype(BF16), rows)

    for dx in range(1, NX):
        send_piece(blocks.at[x, z, c, first_rows, :], send_sem.at[12], fx_recv, at_xy(dx, 0))
    z_piece(0)
    copies[0].wait()
    amp_all[y] = amps_ref[...].astype(BF16)

    copies[4].wait()
    n_items = item_ref.shape[1]
    twice = (iota((n_items, ROWS), 0) == iota((n_items, ROWS), 1) // 2).astype(F32).astype(BF16)
    item = jnp.broadcast_to(item_ref[...].astype(F32), (16, n_items)).astype(BF16)
    row = dot(item, twice)[0:1].astype(jnp.int32)
    square = jnp.broadcast_to(row, (ROWS, ROWS)).astype(F32)
    earlier = (jnp.transpose(square) == square) & (iota((ROWS, ROWS), 0) < iota((ROWS, ROWS), 1))
    rank = jnp.sum(earlier.astype(F32), axis=0, keepdims=True)
    z_of = (row >> 1) & (NZ - 1)
    place = z_of * (BLK8 * CAP) + ((row >> 5) * NC + (row & 1)) * CAP
    slot_all[y] = jnp.broadcast_to(place.astype(F32) + rank, (8, ROWS))

    for i in (5, 6, 7):
        copies[i].wait()
    n_req = owner_ref.shape[1]
    unit = owner_ref[...] * 2 + pair_ref[...]
    hot = (iota((V, n_req), 0) == unit).astype(F32).astype(BF16)
    out_id = iota((16, n_req), 0)
    mine = (iota((16, n_req), 1) // (n_req // 2)) * 2 + mate_ref[...]
    pick = (out_id == mine).astype(F32).astype(BF16)
    counts[x] = dot_nt(pick, hot).astype(BF16)

    for dy in range(1, NY):
        send_piece(slot_all.at[y], send_sem.at[3], s_recv, at_xy(0, dy))
        send_piece(amp_all.at[y], send_sem.at[4], y_recv, at_xy(0, dy))
    for dx in range(1, NX):
        send_piece(counts.at[x], send_sem.at[5], n_recv, at_xy(dx, 0))
    inter_acc[...] = jnp.zeros_like(inter_acc)

    for kind, o in GATHER_ORDER:
        if kind == "slots":
            slot_rows()
        elif kind == "spread":
            spread_counts()
        else:
            {"z": z_piece, "first": first_piece, "x": x_piece, "far": far_piece, "work": block_work}[kind](o)

    for eb in range(N_EB):
        for p in range(2):
            inter[eb, z, c, p] = inter_acc[pl.ds(eb * EB, EB), pl.ds(p * V, V)].astype(BF16)

    def ring_piece(o, eb):
        zz = z_of_piece(o)
        piece = inter.at[eb, zz, c]
        if o:
            await_bytes(piece, g_recv.at[eb, zz])
        for k in sends_of(RING_PLAN, o):
            send_piece(piece, send_sem.at[6], g_recv.at[eb, zz], at_z(k))
        send_piece(piece, send_sem.at[7], gc_recv.at[eb], mate)

    low_lane = iota((EB, 128), 1) < SL

    def sum_part(eb):
        half = UNITS // NC * EB
        sums = dot(spread[c], inter[eb, :, c].reshape(half, V))
        await_bytes(inter.at[eb, :, 1 - c], gc_recv.at[eb])
        sums += dot(spread[1 - c], inter[eb, :, 1 - c].reshape(half, V))
        for xd in range(NX):
            for p in range(2):
                base = (xd * 4 + p * 2) * EB
                first, second = sums[base : base + EB], sums[base + EB : base + 2 * EB]
                for yd in range(NY):
                    t = (yd // 2) * 128
                    f, g = first[:, t : t + 128], second[:, t : t + 128]
                    if yd % 2 == 0:
                        joined = jnp.where(low_lane, f, pltpu.roll(g, SL, 1))
                    else:
                        joined = jnp.where(low_lane, pltpu.roll(f, SL, 1), g)
                    w_send[xd, yd, eb, p] = joined.astype(BF16)
        for dx, dy in offsets:
            there = at_xy(dx, dy)
            remote(
                w_send.at[there["pairs_0"], there["ints"], eb],
                w_recv.at[dx, dy, eb],
                send_sem.at[8 if dx else 10],
                w_rsem.at[1 if dx else 0],
                there,
            ).start()

    for kind, o, eb in RING_ORDER:
        if kind == "ring":
            ring_piece(o, eb)
        else:
            sum_part(eb)

    w_recv[0, 0] = w_send[x, y]
    for i in (1, 8, 9):
        copies[i].wait()
    await_bytes(w_recv.at[0, pl.ds(1, NY - 1)], w_rsem.at[0])
    await_bytes(w_recv.at[pl.ds(1, NX - 1)], w_rsem.at[1])

    lane_low = iota((SL, 128), 1) < SL
    for p in range(2):
        parts = []
        for q in range(NY):
            dy = lax.rem(y - q + NY, NY)
            for eb in range(N_EB):
                parts.append(sum(w_recv[dx, dy, eb, p].astype(F32) for dx in range(NX)))
        w = jnp.transpose(jnp.concatenate(parts, axis=0)).astype(BF16)
        cycle = jnp.zeros((SL, V), F32)
        for j in range(2):
            rows = amp_all[:, pl.ds(j * SL, SL), :].reshape(V, V)
            cycle += dot(w[j * SL : (j + 1) * SL], rows)
        mine_rows = ecol[p, pl.ds(pl.multiple_of(y * SL, SL), SL), :]
        mine_rows = jnp.concatenate([mine_rows, mine_rows], axis=1)
        divisor = mine_rows + energy_ref[p : p + 1, :] - pair_energy_ref[p]
        scaled[p] = (resid[p] + cycle) / divisor
    for q in range(NY):
        t = (q // 2) * 128
        f, g = scaled[0, :, pl.ds(t, 128)], scaled[1, :, pl.ds(t, 128)]
        if q % 2 == 0:
            joined = jnp.where(lane_low, f, pltpu.roll(g, SL, 1))
        else:
            joined = jnp.where(lane_low, pltpu.roll(f, SL, 1), g)
        m_send[q] = joined.astype(BF16)
    for dy in range(NY):
        there = at_xy(NX // 2, dy)
        remote(m_send.at[there["ints"]], m_recv.at[dy], send_sem.at[9], m_rsem, there).start()
    await_bytes(m_recv, m_rsem)
    mirror = jnp.concatenate([m_recv[lax.rem(y - q + NY, NY)].astype(F32) for q in range(NY)], axis=0)
    mirror = jnp.transpose(mirror)
    first_twin = ((xo * NZ + z) * NC + c) * 2
    for p in range(2):
        which = jnp.full((SL, V), twin_ref[p] - first_twin)
        other = jnp.where(which == 1, mirror[SL:], mirror[:SL])
        out_ref[p] = -0.5 * (scaled[p] + other)

    await_bytes(blocks.at[0, pl.ds(0, NZ - 1), 0, rest, :], send_sem.at[0])
    await_bytes(blocks.at[pl.ds(0, NX - 1), :, 0, rest, :], send_sem.at[1])
    await_bytes(blocks.at[:, pl.ds(0, NZ - 1), 0, first_rows, :], send_sem.at[11])
    await_bytes(blocks.at[pl.ds(0, NX - 1), 0, 0, first_rows, :], send_sem.at[12])
    await_bytes(blocks.at[:, :, 0], send_sem.at[2])
    await_bytes(slot_all.at[pl.ds(0, NY - 1)], send_sem.at[3])
    await_bytes(amp_all.at[pl.ds(0, NY - 1)], send_sem.at[4])
    await_bytes(counts.at[pl.ds(0, NX - 1)], send_sem.at[5])
    await_bytes(inter.at[:, pl.ds(0, NZ - 1), 0], send_sem.at[6])
    await_bytes(inter.at[:, :, 0], send_sem.at[7])
    await_bytes(w_recv.at[pl.ds(0, NX - 1)], send_sem.at[8])
    await_bytes(w_recv.at[0, pl.ds(0, NY - 1)], send_sem.at[10])
    await_bytes(m_recv.at[:], send_sem.at[9])


def body(
    amps,
    resid_rest,
    int_blocks,
    virt_energy,
    pair_energy,
    item_block,
    share_owner,
    share_pair,
    share_amp,
    transpose_pair,
):
    n_items, n_req = item_block.shape[0], share_owner.shape[0]
    dma = pltpu.SemaphoreType.DMA
    return pl.pallas_call(
        kernel,
        out_shape=jax.ShapeDtypeStruct((2, SL, V), F32),
        in_specs=[pl.BlockSpec(memory_space=pltpu.HBM)] * 10,
        out_specs=pl.BlockSpec(memory_space=pltpu.VMEM),
        scratch_shapes=[
            pltpu.VMEM((V, V), F32),
            pltpu.VMEM((NX, NZ, NC, SL, V), BF16),
            pltpu.VMEM((NY, ROWS, V), BF16),
            pltpu.VMEM((NY, 8, ROWS), F32),
            pltpu.VMEM((NX, 16, V), BF16),
            pltpu.VMEM((NC, NX * 4 * EB, UNITS // NC * EB), BF16),
            pltpu.VMEM((NZ, SLOTS, 2 * V), BF16),
            pltpu.VMEM((SL, 2 * V), F32),
            pltpu.VMEM((N_EB, NZ, NC, 2, EB, V), BF16),
            pltpu.VMEM((NX, NY, N_EB, 2, EB, 128), BF16),
            pltpu.VMEM((NX, NY, N_EB, 2, EB, 128), BF16),
            pltpu.VMEM((2, SL, V), F32),
            pltpu.VMEM((NY, SL, 128), BF16),
            pltpu.VMEM((NY, SL, 128), BF16),
            pltpu.VMEM((2, V, 128), F32),
            pltpu.VMEM((ROWS, V), F32),
            pltpu.VMEM((2, SL, V), F32),
            pltpu.VMEM((V, V), BF16),
            pltpu.VMEM((2, V), F32),
            pltpu.VMEM((1, n_items), jnp.int32),
            pltpu.VMEM((1, n_req), jnp.int32),
            pltpu.VMEM((1, n_req), jnp.int32),
            pltpu.VMEM((1, n_req), jnp.int32),
            pltpu.SMEM((2,), F32),
            pltpu.SMEM((2,), jnp.int32),
            dma((10,)),
            dma((13,)),
            dma,
            dma,
            dma,
            dma((NZ,)),
            dma((NZ,)),
            dma,
            dma((NZ,)),
            dma((NZ,)),
            dma((NZ,)),
            dma((N_EB, NZ)),
            dma((N_EB,)),
            dma((2,)),
            dma,
        ],
        compiler_params=pltpu.CompilerParams(collective_id=0, has_side_effects=True, vmem_limit_bytes=24 * 2**20),
        name="cycle",
    )(
        *(
            pltpu.with_memory_space_constraint(operand, pltpu.HBM)
            for operand in (
                amps.reshape(ROWS, V),
                resid_rest,
                int_blocks[0],
                virt_energy,
                item_block.reshape(1, -1),
                share_owner.reshape(1, -1),
                share_pair.reshape(1, -1),
                share_amp.reshape(1, -1),
                pair_energy,
                transpose_pair,
            )
        )
    )


def solution(mesh):
    torus = Mesh(
        mesh.devices.reshape(NX, NZ, NC, mesh.shape["ints"]),
        ("pairs_0", "pairs_1", "pairs_2", "ints"),
    )
    return jax.shard_map(
        body,
        mesh=torus,
        in_specs=(
            P(PAIRS, "ints", None),
            P(PAIRS, "ints", None),
            P(PAIRS, None, None),
            P(PAIRS, None),
            P(PAIRS),
            P(PAIRS_INTS, None),
            P(PAIRS, None),
            P(PAIRS, None),
            P(PAIRS, None),
            P(PAIRS),
        ),
        out_specs=P(PAIRS, "ints", None),
        check_vma=False,
    )
```
